128 devices in a mesh: sec: 8 (over y, x_lo), blk: 16 (over x_hi, z, core).
Axes of the slice: x: 4 (x_hi: 2, x_lo: 2; x = x_hi * 2 + x_lo), y: 4, z: 4, core: 2. Of those that a mesh axis runs over, the one named last changes fastest.
Arguments:
- day_solve: bfloat16 [128, 1024, 1024], P(('sec', 'blk')), may hold values from -0.1875 to 0.1875
- couple_invest: bfloat16 [128, 1024, 1024], P(('sec', 'blk')), may hold values from -0.1875 to 0.1875
- invest_blocks: int32 [128, 8], P(('sec', 'blk')), may hold values from 0 to 31, all different within a row
- couple_storage: bfloat16 [128, 1024, 1024], P(('sec', 'blk')), may hold values from -0.015625 to 0.015625
- day_residual: bfloat16 [128, 1024, 256], P(('sec', 'blk')), may hold values from -6 to 6
- directions: bfloat16 [4096, 256], P(('sec', 'blk')), may hold values from -6 to 6
- retention: float32 [128, 1024], P(('sec', 'blk')), may hold values from 0 to 1, as said below
Outputs:
- invest_out: float32 [4096, 256], P(('sec', 'blk'))
- storage_state: bfloat16 [128, 1024, 256], P(('sec', 'blk'))
- day_update: bfloat16 [128, 1024, 256], P(('sec', 'blk'))
The draws below stay inside these ranges and needn't reach their ends.
Inputs may be any that keep to these rules, and one draw needn't show every extreme that they name: `invest_blocks`: each day names 8 different column blocks; every block is named by some day. For each storage state the product of its retention over all 128 days is at most exp(-0.2).
All inputs are finite; a program needn't handle non-finite values.
Results may differ from the reference program's by a relative error of at most 0.012.
Values may be sent and summed in bfloat16 or wider, within the bound.
A program may use at most 512 MiB of HBM per device.

```python
import math
import jax
import jax.numpy as jnp
from jax import lax

INVEST = 4096
BLOCK = 128
COL_BLOCKS = 32
DAY_LINKS = 8
STORAGE_STATES = 1024
ROWS = 1024
TRIALS = 256
YEAR_DAYS = 128


def draw_retention(key, part):
    base_random_key = jax.random.fold_in(key, 11)
    arrival_rate_key, noise_key, surge_key, outage_key = jax.random.split(base_random_key, 4)
    low_rate, high_rate = (0.2, 30.0)
    rates = jnp.exp(jax.random.uniform(arrival_rate_key, (1, STORAGE_STATES), jnp.float32, math.log(low_rate), math.log(high_rate)))
    jitter = jax.random.uniform(noise_key, (YEAR_DAYS, STORAGE_STATES), jnp.float32, 0.5, 2.0)
    steady_level = jnp.exp(-rates * jitter / YEAR_DAYS)
    surge_draws = jax.random.uniform(surge_key, (YEAR_DAYS, STORAGE_STATES), jnp.float32) < 3.0 / YEAR_DAYS
    outage_draws = jax.random.uniform(outage_key, (YEAR_DAYS, STORAGE_STATES), jnp.float32, 0.5, 0.8)
    return jnp.where(surge_draws, steady_level * outage_draws, steady_level).astype(jnp.float32)


def block_scale(stream_key, dims, shards, low, high):
    loudness = 1.0
    for position, parts in shards:
        draws = jax.random.uniform(jax.random.fold_in(jax.random.fold_in(stream_key, 6), position), (parts,), jnp.float32, low / len(shards), high / len(shards))
        loudness = loudness * jnp.repeat(jnp.exp(draws), dims[position] // parts).reshape((-1,) + (1,) * (len(dims) - 1 - position))
    return loudness


def choose_distinct(rng, rows, amount, top, lift):
    ranking = jax.random.permutation(jax.random.fold_in(rng, 1), amount)
    favour = ranking
    for power in range(3):
        favour = favour * favour // amount
    favour = favour * lift // amount
    chance = jax.random.randint(jax.random.fold_in(rng, 2), (rows, amount), 0, 4096) + favour
    fixed_rows = jax.random.permutation(jax.random.fold_in(rng, 3), rows)[jnp.arange(amount) % rows]
    chance = jnp.where(jnp.arange(rows)[:, None] == fixed_rows[None, :], 1 << 14, chance)
    priority = chance * amount + jnp.arange(amount)
    return lax.top_k(priority.astype(jnp.int32), top)[1].astype(jnp.int32)


def scatter_about(own_key, shape, scale, limit, cuts=(), held_as=jnp.bfloat16):
    drawn = jax.random.normal(own_key, shape, jnp.float32) * scale
    if len(cuts) > 0:
        drawn = block_scale(own_key, shape, cuts, -0.22, 0.18) * drawn
    return jnp.clip(drawn, min=-limit, max=limit).astype(held_as)


def setup_inputs(seed: int = 0) -> dict:
    splits = jax.random.split(jax.random.key(seed), 8)
    return {
        "day_solve": scatter_about(splits[0], (YEAR_DAYS, ROWS, ROWS), ROWS ** -0.5, 0.1875, ((0, 128),)),
        "couple_invest": scatter_about(splits[1], (YEAR_DAYS, ROWS, DAY_LINKS * BLOCK), (DAY_LINKS * BLOCK) ** -0.5, 0.1875, ((0, 128),)),
        "invest_blocks": choose_distinct(splits[2], YEAR_DAYS, COL_BLOCKS, DAY_LINKS, 0),
        "couple_storage": scatter_about(splits[3], (YEAR_DAYS, ROWS, STORAGE_STATES), (ROWS * YEAR_DAYS) ** -0.5, 0.015625, ((0, 128),)),
        "day_residual": scatter_about(splits[4], (YEAR_DAYS, ROWS, TRIALS), 1.0, 6.0, ((0, 128),)),
        "directions": scatter_about(splits[5], (INVEST, TRIALS), 1.0, 6.0, ((0, 128),)),
        "retention": draw_retention(jax.random.fold_in(splits[7], 71), 0),
    }


def pick_blocks(directions, block_ids):
    blocks = directions.reshape(INVEST // BLOCK, BLOCK, TRIALS)
    return jnp.take(blocks, block_ids, axis=0).reshape(DAY_LINKS * BLOCK, TRIALS)


def transposed(left_mat, right_mat):
    return lax.dot_general(left_mat, right_mat, (((0,), (0,)), ((), ())), preferred_element_type=jnp.float32)


def reference(day_solve, couple_invest, invest_blocks, couple_storage, day_residual, directions, retention):
    def eliminate(totals, inputs):
        solve_mat, invest_mat, block_ids, storage_mat, residual = inputs
        picked = pick_blocks(directions, block_ids)
        coupled = jnp.dot(invest_mat, picked, preferred_element_type=jnp.float32)
        right_side = (residual.astype(jnp.float32) - coupled).astype(jnp.bfloat16)
        solved = jnp.dot(solve_mat, right_side, preferred_element_type=jnp.float32).astype(jnp.bfloat16)
        portion = transposed(invest_mat, solved).reshape(DAY_LINKS, BLOCK, TRIALS)
        totals = totals.at[block_ids].add(portion)
        inject = transposed(storage_mat, solved)
        return totals, (solved, inject)

    initial = jnp.zeros((INVEST // BLOCK, BLOCK, TRIALS), jnp.float32)
    totals, (solved, inject) = lax.scan(eliminate, initial, (day_solve, couple_invest, invest_blocks, couple_storage, day_residual))
    out_scale = (float(INVEST // BLOCK) / float(YEAR_DAYS * DAY_LINKS)) ** 0.5
    invest_out = totals.reshape(INVEST, TRIALS) * out_scale

    def advance(carried, inputs):
        retain, inject_day = inputs
        return retain[:, None] * carried + inject_day, None

    from_zero, unused = lax.scan(advance, jnp.zeros((STORAGE_STATES, TRIALS), jnp.float32), (retention, inject))
    year_keep = jnp.prod(retention, axis=0)
    opening = from_zero / (1.0 - year_keep)[:, None]

    def replay(carried, inputs):
        retain, inject_day = inputs
        return retain[:, None] * carried + inject_day, carried.astype(jnp.bfloat16)

    unused_end, storage_state = lax.scan(replay, opening, (retention, inject))

    def finish(unused_carry, inputs):
        solve_mat, storage_mat, solved_day, state_day = inputs
        lifted = jnp.dot(storage_mat, state_day, preferred_element_type=jnp.float32).astype(jnp.bfloat16)
        backed = jnp.dot(solve_mat, lifted, preferred_element_type=jnp.float32)
        return unused_carry, (solved_day.astype(jnp.float32) - backed).astype(jnp.bfloat16)

    unused_last, day_update = lax.scan(finish, jnp.zeros((), jnp.float32), (day_solve, couple_storage, solved, storage_state))
    return invest_out, storage_state, day_update
```

```python
import jax
import jax.numpy as jnp
from jax import lax
from jax.experimental import pallas as pl
from jax.experimental.pallas import tpu as pltpu
from jax.sharding import PartitionSpec as P

MESH = pl.DeviceIdType.MESH
F32 = jnp.float32
BF16 = jnp.bfloat16
BLOCKS = 32
LINKS = 8
DAYS = 128
SCALE = (BLOCKS / (DAYS * LINKS)) ** 0.5
X_ORDER = (0, 2, 1, 3)
MESSAGES = 96


def dot(a, b):
    return jnp.dot(a, b, preferred_element_type=F32)


def kernel(
    ds_h, ci_h, ids_h, cs_h, res_h, dir_h, ret_h,
    inv_o, st_o, du_o,
    ds, ci, cs, res, cit, cst, m1, m2, a0, g, picked, solved,
    ids_s, idm_s, idm_v, table,
    ret, rxr, chip_k, kz, kx, ky, col,
    tx_i, own_i, rx_i, day0, tx_p, rx_p, rx_x, rx_y, tx_c, rx_c, tx_s, state,
    por, rx_por, s, half_a, half_b, full_a, full_b, t1, rx2, t2, rx3, inv_v, du_v,
    lsem, ssem, rsem,
):
    sec, blk = lax.axis_index("sec"), lax.axis_index("blk")
    y, x_lo = lax.div(sec, 2), lax.rem(sec, 2)
    x_hi, z, c = lax.div(blk, 8), lax.rem(lax.div(blk, 2), 4), lax.rem(blk, 2)
    x = x_hi * 2 + x_lo
    rank = x_lo * 2 + x_hi
    oc = 1 - c

    def dev(px, py, pz, pc):
        return (py * 2 + lax.rem(px, 2), (lax.div(px, 2) * 4 + pz) * 2 + pc)

    place = {"x": x, "y": y, "z": z}

    def at(axis, k):
        return lax.rem(place[axis] + (k % 4), 4)

    def peer(axis, k):
        q = dict(place)
        q[axis] = at(axis, k)
        return dev(q["x"], q["y"], q["z"], c)

    mate = dev(x, y, z, oc)
    count = [0]
    sends = []
    locals_ = [0]

    def new():
        count[0] += 1
        return count[0] - 1

    def send(m, src, dst, to):
        cp = pltpu.make_async_remote_copy(
            src_ref=src, dst_ref=dst, send_sem=ssem.at[m], recv_sem=rsem.at[m],
            device_id=to, device_id_type=MESH,
        )
        cp.start()
        sends.append(cp)

    def recv(m, dst):
        pltpu.make_async_remote_copy(
            src_ref=dst, dst_ref=dst, send_sem=ssem.at[m], recv_sem=rsem.at[m],
            device_id=mate, device_id_type=MESH,
        ).wait_recv()

    def load(src, dst):
        cp = pltpu.make_async_copy(src, dst, lsem.at[locals_[0]])
        locals_[0] += 1
        cp.start()
        return cp

    own_dir = [
        load(dir_h.at[pl.ds(0, 16)], g.at[c, 0, (y * 4 + x) * 4 + z]),
        load(dir_h.at[pl.ds(16, 16)], g.at[c, 1, (x * 4 + y) * 4 + z]),
    ]
    ret_l = [load(ret_h.at[:, pl.ds(i * 128, 128)], ret.at[i]) for i in range(8)]
    ids_l = load(ids_h, ids_s)
    ds_l = load(ds_h.at[0], ds)
    res_l = load(res_h.at[0], res)
    ci_l = load(ci_h.at[0], ci)
    cs_l = load(cs_h.at[0], cs)

    barrier = pltpu.get_barrier_semaphore()
    for axis in ("x", "y", "z"):
        for k in (1, 2, 3):
            pl.semaphore_signal(barrier, inc=1, device_id=peer(axis, k), device_id_type=MESH)
    pl.semaphore_signal(barrier, inc=1, device_id=mate, device_id_type=MESH)
    pl.semaphore_wait(barrier, 10)

    lead = (y * 4 + x, x * 4 + y)
    first = [[new() for k in range(3)] for h in range(2)]
    for k in (1, 3, 2):
        for h in range(2):
            send(first[h][k - 1], dir_h.at[pl.ds(h * 16, 16)], g.at[c, h, lead[h] * 4 + z], peer("z", k))
    ids_m = new()
    send(ids_m, ids_h, idm_v, mate)
    for cp in ret_l:
        cp.wait()
    ret_m = new()
    send(ret_m, ret, rxr, mate)

    rx_por[8] = jnp.zeros_like(rx_por[8])
    por[0, 8] = jnp.zeros_like(por[0, 8])
    por[1, 8] = jnp.zeros_like(por[1, 8])

    ds_l.wait()
    res_l.wait()

    def a0_tile(i, u):
        r = pl.ds(pl.multiple_of(i * 256, 256), 256)
        a0[r, :] = dot(ds[r, :], res[...])
        return u

    lax.fori_loop(0, 4, a0_tile, 0)

    recv(ret_m, rxr)
    chip_k[...] = ret[...] * rxr[...]
    kz_m = [new() for k in range(3)]
    for k in (1, 2, 3):
        send(kz_m[k - 1], chip_k.at[c * 4 + at("z", k)], kz.at[z], peer("z", k))
    kz[z] = chip_k[c * 4 + z]

    for cp in own_dir:
        cp.wait()
    for h in range(2):
        for k in (1, 3, 2):
            recv(first[h][k - 1], g.at[c, h, lead[h] * 4 + at("z", -k)])

    second = [[new() for k in range(3)] for h in range(2)]
    for k in (1, 3, 2):
        for h, axis in ((0, "x"), (1, "y")):
            rows = pl.ds(lead[h] * 4, 4)
            send(second[h][k - 1], g.at[c, h, rows], g.at[c, h, rows], peer(axis, k))

    ci_l.wait()

    def m1_tile(j, u):
        q = pl.ds(pl.multiple_of(j * 256, 256), 256)
        w = ci[:, q]

        def rows_tile(i, v):
            r = pl.ds(pl.multiple_of(i * 512, 512), 512)
            m1[r, q] = dot(ds[r, :], w).astype(BF16)
            return v

        return lax.fori_loop(0, 2, rows_tile, u)

    lax.fori_loop(0, 2, m1_tile, 0)

    for k in (1, 2, 3):
        recv(kz_m[k - 1], kz.at[at("z", -k)])
    kx[x] = kz[0] * kz[1] * kz[2] * kz[3]
    kx_m = [new() for k in range(3)]
    for k in (1, 2, 3):
        send(kx_m[k - 1], kx.at[x], kx.at[x], peer("x", k))

    for k in (1, 3, 2):
        recv(second[0][k - 1], g.at[c, 0, pl.ds((y * 4 + at("x", -k)) * 4, 4)])
        recv(second[1][k - 1], g.at[c, 1, pl.ds((x * 4 + at("y", -k)) * 4, 4)])

    ring = ("y", "x")
    pos = (y, x)

    def piece(h, p, part):
        return g.at[c, h, pl.ds(p * 16 + part * 8, 8)]

    def block(h, p):
        return g.at[c, h, pl.ds(p * 16, 16)]

    third = [{n: new() for n in ("a+", "a-", "b+", "b-", "f+", "f-")} for h in range(2)]
    for h in range(2):
        send(third[h]["a+"], piece(h, pos[h], 0), piece(h, pos[h], 0), peer(ring[h], 1))
        send(third[h]["a-"], piece(h, pos[h], 1), piece(h, pos[h], 1), peer(ring[h], -1))
    for h in range(2):
        send(third[h]["b+"], piece(h, pos[h], 1), piece(h, pos[h], 1), peer(ring[h], 1))
        send(third[h]["b-"], piece(h, pos[h], 0), piece(h, pos[h], 0), peer(ring[h], -1))
    onchip = [[new() for k in range(4)] for h in range(2)]
    for h in range(2):
        send(onchip[h][0], block(h, pos[h]), block(h, pos[h]), mate)

    lax.fori_loop(2, 3, m1_tile, 0)

    for h in range(2):
        before, after = at(ring[h], -1), at(ring[h], 1)
        recv(third[h]["a+"], piece(h, before, 0))
        send(third[h]["f+"], piece(h, before, 0), piece(h, before, 0), peer(ring[h], 1))
        recv(third[h]["a-"], piece(h, after, 1))
        send(third[h]["f-"], piece(h, after, 1), piece(h, after, 1), peer(ring[h], -1))

    lax.fori_loop(3, 4, m1_tile, 0)

    for k in (1, 2, 3):
        recv(kx_m[k - 1], kx.at[at("x", -k)])
    ky[y] = kx[0] * kx[1] * kx[2] * kx[3]
    ky_m = [new() for k in range(3)]
    for k in (1, 2, 3):
        send(ky_m[k - 1], ky.at[y], ky.at[y], peer("y", k))

    for h in range(2):
        before, after = at(ring[h], -1), at(ring[h], 1)
        recv(third[h]["b+"], piece(h, before, 1))
        send(onchip[h][1], block(h, before), block(h, before), mate)
        recv(third[h]["b-"], piece(h, after, 0))
        send(onchip[h][2], block(h, after), block(h, after), mate)

    cs_l.wait()

    def turn(src, dst):
        def tile(i, u):
            q = pl.ds(pl.multiple_of(i * 128, 128), 128)
            dst[q, :] = src[:, q].T
            return u

        lax.fori_loop(0, 8, tile, 0)

    turn(cs, cst)

    for h in range(2):
        across = at(ring[h], 2)
        recv(third[h]["f+"], piece(h, across, 0))
        recv(third[h]["f-"], piece(h, across, 1))
        send(onchip[h][3], block(h, across), block(h, across), mate)

    turn(ci, cit)

    ids_l.wait()
    recv(ids_m, idm_v)
    load(idm_v, idm_s).wait()

    def place_of(n, u):
        for who, listed in ((0, ids_s), (1, idm_s)):
            found = jnp.int32(8)
            for k in range(LINKS):
                found = jnp.where(listed[0, k] == n, jnp.int32(k), found)
            table[who, n] = found
        return u

    lax.fori_loop(0, BLOCKS, place_of, 0)

    for h in range(2):
        recv(onchip[h][0], g.at[oc, h, pl.ds(pos[h] * 16, 16)])
        recv(onchip[h][1], g.at[oc, h, pl.ds(at(ring[h], -1) * 16, 16)])
        recv(onchip[h][2], g.at[oc, h, pl.ds(at(ring[h], 1) * 16, 16)])
        recv(onchip[h][3], g.at[oc, h, pl.ds(at(ring[h], 2) * 16, 16)])

    def pick(k, u):
        n = ids_s[0, k]
        py, pr, zh = lax.div(n, 8), lax.rem(lax.div(n, 2), 4), lax.rem(n, 2)
        px = lax.rem(pr, 2) * 2 + lax.div(pr, 2)
        for zl in range(2):
            where = ((py * 4 + px) * 4 + zh * 2 + zl, (px * 4 + py) * 4 + zh * 2 + zl)
            for q in range(2):
                for h in range(2):
                    row = pl.multiple_of(k * 128 + zl * 64 + q * 32 + h * 16, 16)
                    picked[pl.ds(row, 16), :] = g[q, h, where[h]]
        return u

    lax.fori_loop(0, LINKS, pick, 0)

    def solve_tile(i, u):
        r = pl.ds(pl.multiple_of(i * 512, 512), 512)
        solved[r, :] = (a0[r, :] - dot(m1[r, :], picked[...])).astype(BF16)
        return u

    lax.fori_loop(0, 2, solve_tile, 0)

    tx_i[...] = dot(cst[pl.ds(pl.multiple_of(oc * 512, 512), 512), :], solved[...]).astype(BF16)
    push_m = new()
    send(push_m, tx_i, rx_i, mate)
    own_i[...] = dot(cst[pl.ds(pl.multiple_of(c * 512, 512), 512), :], solved[...])

    def portion_tile(i, u):
        v = dot(cit[pl.ds(pl.multiple_of(i * 256, 256), 256), :], solved[...]).astype(BF16)
        for kk in range(2):
            for zl in range(2):
                for q in range(2):
                    a = kk * 128 + zl * 64 + q * 32
                    por[q, i * 2 + kk, zl] = v[a : a + 32].reshape(2, 16, 256)
        return u

    lax.fori_loop(0, 4, portion_tile, 0)
    por_m = new()
    send(por_m, por.at[oc, pl.ds(0, 8)], rx_por.at[pl.ds(0, 8)], mate)

    for k in (1, 2, 3):
        recv(ky_m[k - 1], ky.at[at("y", -k)])

    def column(i, v):
        t = jnp.broadcast_to(v, (128, 128)).T
        col[i, :, 0:128] = t
        col[i, :, 128:256] = t

    for i in range(4):
        r_own, r_mate = ret[c * 4 + i], rxr[c * 4 + i]
        r0 = jnp.where(c == 0, r_own, r_mate)
        r1 = jnp.where(c == 0, r_mate, r_own)
        one = jnp.ones_like(r1)
        column(i, kz[i])
        column(4 + i, kx[i])
        column(8 + i, ky[i])
        column(13 + i, r0)
        column(17 + i, jnp.where(c == 0, r1, one))
        column(21 + i, jnp.where(c == 0, one, r1))
    column(12, 1.0 / (1.0 - ky[0] * ky[1] * ky[2] * ky[3]))

    recv(push_m, rx_i)
    for i in range(4):
        r = pl.ds(i * 128, 128)
        mine, theirs = own_i[r, :], rx_i[r, :].astype(F32)
        tx_p[i] = (col[17 + i] * mine + col[21 + i] * theirs).astype(BF16)
        day0[r, :] = jnp.where(c == 0, mine, theirs)
    ring_m = [new() for k in range(3)]
    for k in (2, 1, 3):
        send(ring_m[k - 1], tx_p.at[at("z", k)], rx_p.at[z], peer("z", k))
    rx_p[z] = tx_p[z]

    recv(por_m, rx_por.at[pl.ds(0, 8)])

    def spread(n, u):
        v = por[c, table[0, n]].astype(F32) + rx_por[table[1, n]].astype(F32)
        v = v.astype(BF16)
        py, pr, zh = lax.div(n, 8), lax.rem(lax.div(n, 2), 4), lax.rem(n, 2)
        px = lax.rem(pr, 2) * 2 + lax.div(pr, 2)
        for zl in range(2):
            s[0, px, py, zh * 2 + zl] = v[zl, 0]
            s[1, py, px, zh * 2 + zl] = v[zl, 1]
        return u

    lax.fori_loop(0, BLOCKS, spread, 0)

    axes = ("x", "y")
    r1_m = [{n: new() for n in ("h+", "h-", "f+", "f-")} for h in range(2)]
    for h in range(2):
        far = at(axes[h], 2)
        send(r1_m[h]["h+"], s.at[h, far, pl.ds(0, 2)], half_a.at[h], peer(axes[h], 1))
        send(r1_m[h]["h-"], s.at[h, far, pl.ds(2, 2)], half_b.at[h], peer(axes[h], -1))

    def m2_tile(j):
        w = cs[:, j * 256 : (j + 1) * 256]

        def rows_tile(i, v):
            r = pl.ds(pl.multiple_of(i * 512, 512), 512)
            m2[j // 2, r, (j % 2) * 256 : (j % 2 + 1) * 256] = dot(ds[r, :], w).astype(BF16)
            return v

        lax.fori_loop(0, 2, rows_tile, 0)

    m2_tile(0)

    for k in (1, 3, 2):
        recv(ring_m[k - 1], rx_p.at[at("z", -k)])
    v = rx_p[0].astype(F32)
    for i in (1, 2, 3):
        v = col[i] * v + rx_p[i].astype(F32)
    rx_x[x] = v.astype(BF16)
    row_m = [new() for k in range(3)]
    for k in (2, 1, 3):
        send(row_m[k - 1], rx_x.at[x], rx_x.at[x], peer("x", k))

    for h in range(2):
        nxt, prv = at(axes[h], 1), at(axes[h], -1)
        recv(r1_m[h]["h+"], half_a.at[h])
        s[h, nxt, 0:2] = (s[h, nxt, 0:2].astype(F32) + half_a[h].astype(F32)).astype(BF16)
        send(r1_m[h]["f+"], s.at[h, nxt], full_a.at[h], peer(axes[h], 1))
        recv(r1_m[h]["h-"], half_b.at[h])
        s[h, prv, 2:4] = (s[h, prv, 2:4].astype(F32) + half_b[h].astype(F32)).astype(BF16)
        send(r1_m[h]["f-"], s.at[h, prv], full_b.at[h], peer(axes[h], -1))

    m2_tile(1)

    for k in (1, 3, 2):
        recv(row_m[k - 1], rx_x.at[at("x", -k)])
    v = rx_x[0].astype(F32)
    for i in X_ORDER[1:]:
        v = col[4 + i] * v + rx_x[i].astype(F32)
    rx_y[y] = v.astype(BF16)
    yr_m = [new() for k in range(3)]
    for k in (2, 1, 3):
        send(yr_m[k - 1], rx_y.at[y], rx_y.at[y], peer("y", k))

    m2_tile(2)

    axes2 = ("y", "x")
    r2_m = [[new() for k in range(3)] for h in range(2)]
    for h in range(2):
        recv(r1_m[h]["f+"], full_a.at[h])
        recv(r1_m[h]["f-"], full_b.at[h])
        mine = (x, y)[h]
        t1[h] = (s[h, mine].astype(F32) + full_a[h].astype(F32) + full_b[h].astype(F32)).astype(BF16)
        for k in (2, 1, 3):
            send(r2_m[h][k - 1], t1.at[h, at(axes2[h], k)], rx2.at[h, k - 1], peer(axes2[h], k))

    for k in (1, 3, 2):
        recv(yr_m[k - 1], rx_y.at[at("y", -k)])
    v = rx_y[0].astype(F32)
    for i in (1, 2, 3):
        v = col[8 + i] * v + rx_y[i].astype(F32)
    v = v * col[12]
    for i in range(4):
        v = jnp.where(i < y, col[8 + i] * v + rx_y[i].astype(F32), v)
    for j, i in enumerate(X_ORDER):
        v = jnp.where(j < rank, col[4 + i] * v + rx_x[i].astype(F32), v)
    for i in range(4):
        tx_c[i] = v.astype(BF16)
        if i < 3:
            v = col[i] * v + rx_p[i].astype(F32)
    back_m = [new() for k in range(3)]
    for k in (2, 1, 3):
        send(back_m[k - 1], tx_c.at[at("z", k)], rx_c.at[z], peer("z", k))
    rx_c[z] = tx_c[z]

    m2_tile(3)

    r3_m = [[new() for k in range(3)] for h in range(2)]
    for h in range(2):
        v = t1[h, pos[h]].astype(F32)
        for k in (1, 3, 2):
            recv(r2_m[h][k - 1], rx2.at[h, k - 1])
            v = v + rx2[h, k - 1].astype(F32)
        t2[h] = v.astype(BF16)
        for k in (2, 1, 3):
            send(r3_m[h][k - 1], t2.at[h, at("z", k)], rx3.at[h, k - 1], peer("z", k))

    for k in (1, 3, 2):
        recv(back_m[k - 1], rx_c.at[at("z", -k)])
    for i in range(4):
        r = pl.ds(i * 128, 128)
        u = rx_c[i].astype(F32)
        w = col[13 + i] * u + day0[r, :]
        state[c, r, :] = jnp.where(c == 0, u, w).astype(BF16)
        tx_s[r, :] = jnp.where(c == 0, w, u).astype(BF16)
    swap_m = new()
    send(swap_m, tx_s, state.at[c], mate)
    outs = [load(state.at[c], st_o.at[0, pl.ds(pl.multiple_of(c * 512, 512), 512), :])]

    def back_own(i, u):
        r = pl.ds(pl.multiple_of(i * 512, 512), 512)
        a0[r, :] = solved[r, :].astype(F32) - dot(m2[c, r, :], state[c])
        return u

    lax.fori_loop(0, 2, back_own, 0)

    for h in range(2):
        v = t2[h, z].astype(F32)
        for k in (1, 3, 2):
            recv(r3_m[h][k - 1], rx3.at[h, k - 1])
            v = v + rx3[h, k - 1].astype(F32)
        inv_v[h * 16 : (h + 1) * 16, :] = v * SCALE
    outs.append(load(inv_v, inv_o))

    recv(swap_m, state.at[oc])
    outs.append(load(state.at[oc], st_o.at[0, pl.ds(pl.multiple_of(oc * 512, 512), 512), :]))
    for i in range(2):
        r = pl.ds(i * 512, 512)
        du_v[r, :] = (a0[r, :] - dot(m2[oc, r, :], state[oc])).astype(BF16)
        outs.append(load(du_v.at[r], du_o.at[0, r, :]))

    for cp in sends:
        cp.wait_send()
    for cp in outs:
        cp.wait()


def body(*arrays):
    hbm = pl.BlockSpec(memory_space=pl.ANY)
    v = pltpu.VMEM
    scratch = [
        v((1024, 1024), BF16), v((1024, 1024), BF16), v((1024, 1024), BF16), v((1024, 256), BF16),
        v((1024, 1024), BF16), v((1024, 1024), BF16), v((1024, 1024), BF16), v((2, 1024, 512), BF16),
        v((1024, 256), F32), v((2, 2, 64, 16, 256), BF16), v((1024, 256), BF16), v((1024, 256), BF16),
        pltpu.SMEM((1, 8), jnp.int32), pltpu.SMEM((1, 8), jnp.int32), v((1, 8), jnp.int32),
        pltpu.SMEM((2, 32), jnp.int32),
        v((8, 1, 128), F32), v((8, 1, 128), F32), v((8, 1, 128), F32),
        v((4, 1, 128), F32), v((4, 1, 128), F32), v((4, 1, 128), F32), v((25, 128, 256), F32),
        v((512, 256), BF16), v((512, 256), F32), v((512, 256), BF16), v((512, 256), F32),
        v((4, 128, 256), BF16), v((4, 128, 256), BF16), v((4, 128, 256), BF16), v((4, 128, 256), BF16),
        v((4, 128, 256), BF16), v((4, 128, 256), BF16), v((512, 256), BF16), v((2, 512, 256), BF16),
        v((2, 9, 2, 2, 16, 256), BF16), v((9, 2, 2, 16, 256), BF16), v((2, 4, 4, 4, 16, 256), BF16),
        v((2, 2, 4, 16, 256), BF16), v((2, 2, 4, 16, 256), BF16),
        v((2, 4, 4, 16, 256), BF16), v((2, 4, 4, 16, 256), BF16), v((2, 4, 4, 16, 256), BF16),
        v((2, 3, 4, 16, 256), BF16), v((2, 4, 16, 256), BF16), v((2, 3, 16, 256), BF16),
        v((32, 256), F32), v((1024, 256), BF16),
        pltpu.SemaphoreType.DMA((32,)), pltpu.SemaphoreType.DMA((MESSAGES,)), pltpu.SemaphoreType.DMA((MESSAGES,)),
    ]
    return pl.pallas_call(
        kernel,
        out_shape=(
            jax.ShapeDtypeStruct((32, 256), F32),
            jax.ShapeDtypeStruct((1, 1024, 256), BF16),
            jax.ShapeDtypeStruct((1, 1024, 256), BF16),
        ),
        in_specs=[hbm] * 7,
        out_specs=(hbm,) * 3,
        scratch_shapes=scratch,
        compiler_params=pltpu.CompilerParams(
            collective_id=0, has_side_effects=True, vmem_limit_bytes=60 * 1024 * 1024
        ),
    )(*arrays)


def solution(mesh):
    days = ("sec", "blk")
    in_specs = (
        P(days, None, None), P(days, None, None), P(days, None), P(days, None, None),
        P(days, None, None), P(days, None), P(days, None),
    )
    out_specs = (P(days, None), P(days, None, None), P(days, None, None))
    return jax.shard_map(body, mesh=mesh, in_specs=in_specs, out_specs=out_specs, check_vma=False)
```

```python
import jax
import jax.numpy as jnp
from jax import lax
from jax.experimental import pallas as pl
from jax.experimental.pallas import tpu as pltpu
from jax.sharding import PartitionSpec as P

MESH = pl.DeviceIdType.MESH
F32 = jnp.float32
BF16 = jnp.bfloat16
BLOCKS = 32
LINKS = 8
DAYS = 128
SCALE = (BLOCKS / (DAYS * LINKS)) ** 0.5
MESSAGES = 64


def dot(a, b):
    return jnp.dot(a, b, preferred_element_type=F32)


def kernel(
    ds_h, ci_h, ids_h, cs_h, res_h, dir_h, ret_h,
    inv_v, state, du_v,
    ds, ci, cs, res, cit, cst, m1, m2, a0, g, picked, solved,
    ids_s, idm_s, idm_v, table,
    ret, rxr, kall, kmat, kcol, kseg, col,
    tx_i, own_i, rx_i, day0, tx_p, rx_p, tx_c, rx_c, tx_s,
    por, rx_por, s, full, t1, rx2,
    lsem, ssem, rsem,
):
    sec, blk = lax.axis_index("sec"), lax.axis_index("blk")
    y, x_lo = lax.div(sec, 2), lax.rem(sec, 2)
    x_hi, z, c = lax.div(blk, 8), lax.rem(lax.div(blk, 2), 4), lax.rem(blk, 2)
    x = x_hi * 2 + x_lo
    rank = x_lo * 2 + x_hi
    oc = 1 - c
    here = (y * 4 + rank) * 4 + z

    xs, ys, zs = ([lax.rem(v + k, 4) for k in range(4)] for v in (x, y, z))
    x_sec, x_blk = [lax.rem(v, 2) for v in xs], [lax.div(v, 2) * 8 + c for v in xs]
    y_sec, z_blk = [v * 2 for v in ys], [v * 2 for v in zs]
    x_rank = [lax.rem(v, 2) * 2 + lax.div(v, 2) for v in xs]
    x_at, y_at = [v * 4 for v in x_rank], [v * 16 for v in ys]

    def peer(dx, dy, dz):
        return (y_sec[dy % 4] + x_sec[dx % 4], x_blk[dx % 4] + z_blk[dz % 4])

    def year(dx, dy, dz):
        return y_at[dy % 4] + x_at[dx % 4] + zs[dz % 4]

    def far(d):
        return -sum(min(v, 4 - v) for v in d)

    mate = (sec, blk + 1 - 2 * c)
    count = [0]
    sends = []
    local = [0]

    def new():
        count[0] += 1
        return count[0] - 1

    def copy(m, src, dst, to):
        return pltpu.make_async_remote_copy(
            src_ref=src, dst_ref=dst, send_sem=ssem.at[m], recv_sem=rsem.at[m],
            device_id=to, device_id_type=MESH,
        )

    def send(m, src, dst, to, whole=None):
        cp = copy(m, src, dst, to)
        cp.start()
        if whole is None:
            sends.append(cp)

    def sent(m, whole):
        sends.append(copy(m, whole, whole, mate))

    def recv(m, dst):
        copy(m, dst, dst, mate).wait_recv()

    def load(src, dst):
        cp = pltpu.make_async_copy(src, dst, lsem.at[local[0]])
        local[0] += 1
        cp.start()
        return cp

    lead = (y * 4 + x, x * 4 + y)
    own = [g.at[c, h, lead[h] * 4 + z] for h in range(2)]
    own_dir = [load(dir_h.at[pl.ds(h * 16, 16)], own[h]) for h in range(2)]
    ret_l = [load(ret_h.at[:, pl.ds(i * 128, 128)], ret.at[i]) for i in range(8)]
    ids_l = load(ids_h, ids_s)
    ds_l = load(ds_h.at[0], ds)
    res_l = load(res_h.at[0], res)
    ci_l = load(ci_h.at[0], ci)
    cs_l = load(cs_h.at[0], cs)

    plane = sorted([(i, j) for i in range(4) for j in range(4) if i or j], key=far)
    flat = sorted(
        [(i, j, k) for i in range(4) for j in range(4) for k in range(4) if i or j or k], key=far
    )
    greet = [d for d in flat if d[0] == 0 or d[1] == 0]
    barrier = pltpu.get_barrier_semaphore()
    for d in greet:
        pl.semaphore_signal(barrier, inc=1, device_id=peer(*d), device_id_type=MESH)
    pl.semaphore_signal(barrier, inc=1, device_id=mate, device_id_type=MESH)
    for cp in own_dir:
        cp.wait()
    pl.semaphore_wait(barrier, len(greet) + 1)

    first = [[new() for k in range(4)] for h in range(2)]
    for d, dz in plane:
        send(first[0][d], own[0], own[0], peer(d, 0, dz), True)
        send(first[1][d], own[1], own[1], peer(0, d, dz), True)
    for h in range(2):
        for d in range(4):
            sent(first[h][d], g.at[c, h, pl.ds(0, 3 if d == 0 else 4)])

    ids_m = new()
    send(ids_m, ids_h, idm_v, mate)
    for cp in ret_l:
        cp.wait()
    ret_m = new()
    send(ret_m, ret, rxr, mate)

    rx_por[8] = jnp.zeros_like(rx_por[8])
    por[0, 8] = jnp.zeros_like(por[0, 8])
    por[1, 8] = jnp.zeros_like(por[1, 8])

    recv(ret_m, rxr)
    for i in range(4):
        kall[y, rank, z, i] = ret[c * 4 + i] * rxr[c * 4 + i]
    kz_m = [new() for k in range(3)]
    for k in (2, 1, 3):
        send(kz_m[k - 1], kall.at[y, rank, z], kall.at[y, rank, z], peer(0, 0, k))

    own_line = (xs, ys)
    second = [[new() for k in range(3)] for h in range(2)]

    def line(h, v, d):
        return g.at[c, h, pl.ds((v * 4 + own_line[h][-d % 4]) * 4, 4)]

    def third(h, k):
        return peer(0, k, 0) if h == 0 else peer(k, 0, 0)

    me = (y, x)
    for d in (0, 1, 3, 2):
        for h in range(2):
            if d == 0:
                recv(first[h][0], g.at[c, h, pl.ds(0, 3)])
            else:
                recv(first[h][d], line(h, me[h], d))
            for k in (2, 1, 3):
                send(second[h][k - 1], line(h, me[h], d), line(h, me[h], d), third(h, k), True)
    across = (ys, xs)

    def block(p, h, v):
        return g.at[p, h, pl.ds(v * 16, 16)]

    for h in range(2):
        for k in range(3):
            sent(second[h][k], block(c, h, 0))
    onchip = [[new() for k in range(4)] for h in range(2)]
    for h in range(2):
        send(onchip[h][0], block(c, h, me[h]), block(c, h, me[h]), mate)

    for k in (1, 3, 2):
        recv(kz_m[k - 1], kall.at[y, rank, zs[-k % 4]])
    kx_m = [new() for k in range(3)]
    for k in (2, 1, 3):
        send(kx_m[k - 1], kall.at[y, rank], kall.at[y, rank], peer(k, 0, 0))

    ds_l.wait()
    res_l.wait()

    def a0_tile(i, u):
        r = pl.ds(pl.multiple_of(i * 256, 256), 256)
        a0[r, :] = dot(ds[r, :], res[...])
        return u

    lax.fori_loop(0, 4, a0_tile, 0)
    ci_l.wait()

    def m1_tile(j, u):
        q = pl.ds(pl.multiple_of(j * 256, 256), 256)
        w = ci[:, q]

        def rows_tile(i, v):
            r = pl.ds(pl.multiple_of(i * 512, 512), 512)
            m1[r, q] = dot(ds[r, :], w).astype(BF16)
            return v

        return lax.fori_loop(0, 2, rows_tile, u)

    lax.fori_loop(0, 3, m1_tile, 0)

    for k in (1, 3, 2):
        recv(kx_m[k - 1], kall.at[y, x_rank[-k % 4]])
    ky_m = [new() for k in range(3)]
    for k in (2, 1, 3):
        send(ky_m[k - 1], kall.at[y], kall.at[y], peer(0, k, 0))

    for k in (1, 3):
        for h in range(2):
            v = across[h][-k % 4]
            recv(second[h][k - 1], block(c, h, v))
            send(onchip[h][k], block(c, h, v), block(c, h, v), mate)

    lax.fori_loop(3, 4, m1_tile, 0)

    for h in range(2):
        v = across[h][2]
        recv(second[h][1], block(c, h, v))
        send(onchip[h][2], block(c, h, v), block(c, h, v), mate)

    cs_l.wait()

    def turn(src, dst):
        def tile(i, u):
            q = pl.ds(pl.multiple_of(i * 128, 128), 128)
            dst[q, :] = src[:, q].T
            return u

        lax.fori_loop(0, 8, tile, 0)

    turn(cs, cst)

    ids_l.wait()
    recv(ids_m, idm_v)
    load(idm_v, idm_s).wait()

    def place_of(n, u):
        for who, listed in ((0, ids_s), (1, idm_s)):
            found = jnp.int32(8)
            for k in range(LINKS):
                found = jnp.where(listed[0, k] == n, jnp.int32(k), found)
            table[who, n] = found
        return u

    lax.fori_loop(0, BLOCKS, place_of, 0)

    for k in (0, 1, 3, 2):
        for h in range(2):
            recv(onchip[h][k], block(oc, h, across[h][-k % 4]))

    def pick(k, u):
        n = ids_s[0, k]
        py, pr, zh = lax.div(n, 8), lax.rem(lax.div(n, 2), 4), lax.rem(n, 2)
        px = lax.rem(pr, 2) * 2 + lax.div(pr, 2)
        for zl in range(2):
            where = ((py * 4 + px) * 4 + zh * 2 + zl, (px * 4 + py) * 4 + zh * 2 + zl)
            for q in range(2):
                for h in range(2):
                    row = pl.multiple_of(k * 128 + zl * 64 + q * 32 + h * 16, 16)
                    picked[pl.ds(row, 16), :] = g[q, h, where[h]]
        return u

    lax.fori_loop(0, LINKS, pick, 0)

    def solve_tile(i, u):
        r = pl.ds(pl.multiple_of(i * 512, 512), 512)
        solved[r, :] = (a0[r, :] - dot(m1[r, :], picked[...])).astype(BF16)
        return u

    lax.fori_loop(0, 2, solve_tile, 0)

    tx_i[...] = dot(cst[pl.ds(pl.multiple_of(oc * 512, 512), 512), :], solved[...]).astype(BF16)
    push_m = new()
    send(push_m, tx_i, rx_i, mate)
    own_i[...] = dot(cst[pl.ds(pl.multiple_of(c * 512, 512), 512), :], solved[...])

    def column(i, v):
        col[i] = jnp.broadcast_to(v, (128, 128)).T

    for i in range(4):
        r_own, r_mate = ret[c * 4 + i], rxr[c * 4 + i]
        r0 = jnp.where(c == 0, r_own, r_mate)
        r1 = jnp.where(c == 0, r_mate, r_own)
        one = jnp.ones_like(r1)
        column(i, r0)
        column(4 + i, jnp.where(c == 0, r1, one))
        column(8 + i, jnp.where(c == 0, one, r1))

    recv(push_m, rx_i)
    for i in range(4):
        r = pl.ds(i * 128, 128)
        for q in range(2):
            w = pl.ds(q * 128, 128)
            mine, theirs = own_i[r, w], rx_i[r, w].astype(F32)
            v = (col[4 + i] * mine + col[8 + i] * theirs).astype(BF16)
            for j in range(8):
                tx_p[(i * 8 + j) * 2 + q] = v[j * 16 : (j + 1) * 16]
            day0[r, w] = jnp.where(c == 0, mine, theirs)
    year_m = new()
    for d in flat:
        send(year_m, tx_p.at[year(*d)], rx_p.at[here], peer(*d), True)
    sent(year_m, rx_p.at[pl.ds(0, 63)])
    rx_p[here] = tx_p[here]

    turn(ci, cit)

    def portion_tile(i, u):
        v = dot(cit[pl.ds(pl.multiple_of(i * 256, 256), 256), :], solved[...]).astype(BF16)
        for kk in range(2):
            for zl in range(2):
                for q in range(2):
                    a = kk * 128 + zl * 64 + q * 32
                    por[q, i * 2 + kk, zl] = v[a : a + 32].reshape(2, 16, 256)
        return u

    lax.fori_loop(0, 4, portion_tile, 0)
    por_m = new()
    send(por_m, por.at[oc, pl.ds(0, 8)], rx_por.at[pl.ds(0, 8)], mate)

    for k in (1, 3, 2):
        recv(ky_m[k - 1], kall.at[ys[-k % 4]])
    for i in range(64):
        kmat[0, i : i + 1, :] = kall[i // 16, i // 4 % 4, i % 4, y]
    kmat[0, 64:128, :] = jnp.zeros((64, 128), F32)
    kmat[1] = kmat[0].T
    mine = kmat[1, pl.ds(pl.multiple_of((rank * 2 + lax.div(z, 2)) * 16, 16), 16), :]
    for i in range(64):
        kcol[i] = jnp.broadcast_to(mine[:, i : i + 1], (16, 128))
    total = None
    for i in range(8):
        v = kcol[i * 8]
        for j in range(1, 8):
            v = v * kcol[i * 8 + j]
        kseg[i] = v
        total = v if total is None else total * v
    kseg[8] = 1.0 / (1.0 - total)

    recv(por_m, rx_por.at[pl.ds(0, 8)])

    def spread(n, u):
        v = por[c, table[0, n]].astype(F32) + rx_por[table[1, n]].astype(F32)
        v = v.astype(BF16)
        py, pr, zh = lax.div(n, 8), lax.rem(lax.div(n, 2), 4), lax.rem(n, 2)
        px = lax.rem(pr, 2) * 2 + lax.div(pr, 2)
        for zl in range(2):
            s[0, px, py, zh * 2 + zl] = v[zl, 0]
            s[1, py, px, zh * 2 + zl] = v[zl, 1]
        return u

    lax.fori_loop(0, BLOCKS, spread, 0)

    r1_m = [[new() for k in range(3)] for h in range(2)]
    for k in (2, 1, 3):
        for h in range(2):
            to = peer(k, 0, 0) if h == 0 else peer(0, k, 0)
            send(r1_m[h][k - 1], s.at[h, (xs, ys)[h][k]], full.at[h, k - 1], to)

    recv(year_m, rx_p.at[pl.ds(0, 63)])
    runs = []
    for i in range(8):
        v = rx_p[i * 8].astype(F32)
        for j in range(1, 8):
            v = kcol[i * 8 + j] * v + rx_p[i * 8 + j].astype(F32)
        runs.append(v)
    v = runs[0]
    for i in range(1, 8):
        v = kseg[i] * v + runs[i]
    v = v * kseg[8]
    starts = []
    for i in range(8):
        starts.append(v)
        v = kseg[i] * v + runs[i]
    for i in range(8):
        v = starts[i]
        for j in range(8):
            tx_c[i * 8 + j] = v.astype(BF16)
            if j < 7:
                v = kcol[i * 8 + j] * v + rx_p[i * 8 + j].astype(F32)
    back_m = new()
    for d in flat:
        send(back_m, tx_c.at[year(*d)], rx_c.at[here], peer(*d), True)
    sent(back_m, rx_c.at[pl.ds(0, 63)])
    rx_c[here] = tx_c[here]

    def m2_tile(j):
        w = cs[:, j * 256 : (j + 1) * 256]

        def rows_tile(i, v):
            r = pl.ds(pl.multiple_of(i * 512, 512), 512)
            m2[j // 2, r, (j % 2) * 256 : (j % 2 + 1) * 256] = dot(ds[r, :], w).astype(BF16)
            return v

        lax.fori_loop(0, 2, rows_tile, 0)

    m2_tile(0)
    m2_tile(1)

    r2_m = [new() for h in range(2)]
    for h in range(2):
        v = s[h, me[1 - h]].astype(F32)
        for k in (1, 3, 2):
            recv(r1_m[h][k - 1], full.at[h, k - 1])
            v = v + full[h, k - 1].astype(F32)
        t1[h] = v.astype(BF16)
        for d, dz in plane:
            to = peer(0, d, dz) if h == 0 else peer(d, 0, dz)
            send(r2_m[h], t1.at[h, across[h][d], zs[dz]], rx2.at[h, d * 4 + dz], to, True)
        sent(r2_m[h], rx2.at[h, pl.ds(1, 15)])

    m2_tile(2)
    m2_tile(3)

    recv(back_m, rx_c.at[pl.ds(0, 63)])
    for i in range(4):
        for j in range(8):
            for q in range(2):
                a = i * 128 + j * 16
                r, w = pl.ds(a, 16), pl.ds(q * 128, 128)
                u = rx_c[(i * 8 + j) * 2 + q].astype(F32)
                v = col[i, j * 16 : (j + 1) * 16, :] * u + day0[r, w]
                state[c, r, w] = jnp.where(c == 0, u, v).astype(BF16)
                tx_s[r, w] = jnp.where(c == 0, v, u).astype(BF16)
    swap_m = new()
    send(swap_m, tx_s, state.at[c], mate)

    def back_own(i, u):
        r = pl.ds(pl.multiple_of(i * 512, 512), 512)
        a0[r, :] = solved[r, :].astype(F32) - dot(m2[c, r, :], state[c])
        return u

    lax.fori_loop(0, 2, back_own, 0)

    for h in range(2):
        recv(r2_m[h], rx2.at[h, pl.ds(1, 15)])
        v = t1[h, me[h], z].astype(F32)
        for k in range(1, 16):
            v = v + rx2[h, k].astype(F32)
        inv_v[h * 16 : (h + 1) * 16, :] = v * SCALE

    recv(swap_m, state.at[oc])
    for i in range(2):
        r = pl.ds(i * 512, 512)
        du_v[r, :] = (a0[r, :] - dot(m2[oc, r, :], state[oc])).astype(BF16)

    for cp in sends:
        cp.wait_send()


def body(*arrays):
    hbm = pl.BlockSpec(memory_space=pl.ANY)
    v = pltpu.VMEM
    scratch = [
        v((1024, 1024), BF16), v((1024, 1024), BF16), v((1024, 1024), BF16), v((1024, 256), BF16),
        v((1024, 1024), BF16), v((1024, 1024), BF16), v((1024, 1024), BF16), v((2, 1024, 512), BF16),
        v((1024, 256), F32), v((2, 2, 64, 16, 256), BF16), v((1024, 256), BF16), v((1024, 256), BF16),
        pltpu.SMEM((1, 8), jnp.int32), pltpu.SMEM((1, 8), jnp.int32), v((1, 8), jnp.int32),
        pltpu.SMEM((2, 32), jnp.int32),
        v((8, 1, 128), F32), v((8, 1, 128), F32), v((4, 4, 4, 4, 1, 128), F32),
        v((2, 128, 128), F32), v((64, 16, 128), F32), v((9, 16, 128), F32), v((12, 128, 128), F32),
        v((512, 256), BF16), v((512, 256), F32), v((512, 256), BF16), v((512, 256), F32),
        v((64, 16, 128), BF16), v((64, 16, 128), BF16), v((64, 16, 128), BF16), v((64, 16, 128), BF16),
        v((512, 256), BF16),
        v((2, 9, 2, 2, 16, 256), BF16), v((9, 2, 2, 16, 256), BF16), v((2, 4, 4, 4, 16, 256), BF16),
        v((2, 3, 4, 4, 16, 256), BF16), v((2, 4, 4, 16, 256), BF16), v((2, 16, 16, 256), BF16),
        pltpu.SemaphoreType.DMA((32,)), pltpu.SemaphoreType.DMA((MESSAGES,)), pltpu.SemaphoreType.DMA((MESSAGES,)),
    ]
    inv, state, du = pl.pallas_call(
        kernel,
        out_shape=(v((32, 256), F32), v((2, 512, 256), BF16), v((1024, 256), BF16)),
        in_specs=[hbm] * 7,
        out_specs=(pl.BlockSpec(memory_space=v),) * 3,
        scratch_shapes=scratch,
        compiler_params=pltpu.CompilerParams(
            collective_id=0, has_side_effects=True, vmem_limit_bytes=60 * 1024 * 1024
        ),
    )(*arrays)
    return pl.pallas_call(
        deliver,
        out_shape=(
            jax.ShapeDtypeStruct((32, 256), F32),
            jax.ShapeDtypeStruct((1, 1024, 256), BF16),
            jax.ShapeDtypeStruct((1, 1024, 256), BF16),
        ),
        in_specs=[pl.BlockSpec(memory_space=v)] * 3,
        out_specs=(hbm,) * 3,
        scratch_shapes=[pltpu.SemaphoreType.DMA((4,))],
        compiler_params=pltpu.CompilerParams(vmem_limit_bytes=8 * 1024 * 1024),
    )(inv, state, du)


def deliver(inv_v, state, du_v, inv_o, st_o, du_o, sem):
    cps = [
        pltpu.make_async_copy(state.at[0], st_o.at[0, pl.ds(0, 512), :], sem.at[0]),
        pltpu.make_async_copy(state.at[1], st_o.at[0, pl.ds(512, 512), :], sem.at[1]),
        pltpu.make_async_copy(du_v, du_o.at[0], sem.at[2]),
        pltpu.make_async_copy(inv_v, inv_o, sem.at[3]),
    ]
    for cp in cps:
        cp.start()
    for cp in cps:
        cp.wait()


def solution(mesh):
    days = ("sec", "blk")
    in_specs = (
        P(days, None, None), P(days, None, None), P(days, None), P(days, None, None),
        P(days, None, None), P(days, None), P(days, None),
    )
    out_specs = (P(days, None), P(days, None, None), P(days, None, None))
    return jax.shard_map(body, mesh=mesh, in_specs=in_specs, out_specs=out_specs, check_vma=False)
```

```python
import jax
import jax.numpy as jnp
from jax import lax
from jax.experimental import pallas as pl
from jax.experimental.pallas import tpu as pltpu
from jax.sharding import PartitionSpec as P

MESH = pl.DeviceIdType.MESH
F32 = jnp.float32
BF16 = jnp.bfloat16
BLOCKS = 32
LINKS = 8
DAYS = 128
SCALE = (BLOCKS / (DAYS * LINKS)) ** 0.5
MESSAGES = 64


def dot(a, b):
    return jnp.dot(a, b, preferred_element_type=F32)


def kernel(
    ds_h, ci_h, ids_h, cs_h, res_h, dir_h, ret_h,
    inv_v, state, du_v,
    ds, ci, cs, res, cit, cst, m1, m2, a0, a0b, b, bm, ca, cam, pm, pmm, pa, pam, g, picked, solved,
    ids_s, idm_s, idm_v, table,
    ret, rxr, kall, kmat, kcol, kseg, col,
    own_i, rx_i, day0, tx_p, rx_p, tx_c, rx_c, tx_s,
    por, rx_por, s, full, t1, rx2,
    lsem, ssem, rsem,
):
    sec, blk = lax.axis_index("sec"), lax.axis_index("blk")
    y, x_lo = lax.div(sec, 2), lax.rem(sec, 2)
    x_hi, z, c = lax.div(blk, 8), lax.rem(lax.div(blk, 2), 4), lax.rem(blk, 2)
    x = x_hi * 2 + x_lo
    rank = x_lo * 2 + x_hi
    oc = 1 - c
    here = (y * 4 + rank) * 4 + z

    xs, ys, zs = ([lax.rem(v + k, 4) for k in range(4)] for v in (x, y, z))
    x_sec, x_blk = [lax.rem(v, 2) for v in xs], [lax.div(v, 2) * 8 + c for v in xs]
    y_sec, z_blk = [v * 2 for v in ys], [v * 2 for v in zs]
    x_rank = [lax.rem(v, 2) * 2 + lax.div(v, 2) for v in xs]
    x_at, y_at = [v * 4 for v in x_rank], [v * 16 for v in ys]

    def peer(dx, dy, dz):
        return (y_sec[dy % 4] + x_sec[dx % 4], x_blk[dx % 4] + z_blk[dz % 4])

    def year(dx, dy, dz):
        return y_at[dy % 4] + x_at[dx % 4] + zs[dz % 4]

    def far(d):
        return -sum(min(v, 4 - v) for v in d)

    mate = (sec, blk + 1 - 2 * c)
    count = [0]
    sends = []
    local = [0]

    def new():
        count[0] += 1
        return count[0] - 1

    def copy(m, src, dst, to):
        return pltpu.make_async_remote_copy(
            src_ref=src, dst_ref=dst, send_sem=ssem.at[m], recv_sem=rsem.at[m],
            device_id=to, device_id_type=MESH,
        )

    def send(m, src, dst, to, whole=None):
        cp = copy(m, src, dst, to)
        cp.start()
        if whole is None:
            sends.append(cp)

    def sent(m, whole):
        sends.append(copy(m, whole, whole, mate))

    def recv(m, dst):
        copy(m, dst, dst, mate).wait_recv()

    def load(src, dst):
        cp = pltpu.make_async_copy(src, dst, lsem.at[local[0]])
        local[0] += 1
        cp.start()
        return cp

    lead = (y * 4 + x, x * 4 + y)
    own = [g.at[c, h, lead[h] * 4 + z] for h in range(2)]
    own_dir = [load(dir_h.at[pl.ds(h * 16, 16)], own[h]) for h in range(2)]
    ret_l = [load(ret_h.at[:, pl.ds(i * 128, 128)], ret.at[i]) for i in range(8)]
    ids_l = load(ids_h, ids_s)
    ds_l = load(ds_h.at[0], ds)
    res_l = load(res_h.at[0], res)
    ci_l = load(ci_h.at[0], ci)
    cs_l = load(cs_h.at[0], cs)

    plane = sorted([(i, j) for i in range(4) for j in range(4) if i or j], key=far)
    flat = sorted(
        [(i, j, k) for i in range(4) for j in range(4) for k in range(4) if i or j or k], key=far
    )
    greet = [d for d in flat if d[0] == 0 or d[1] == 0]
    barrier = pltpu.get_barrier_semaphore()
    for d in greet:
        pl.semaphore_signal(barrier, inc=1, device_id=peer(*d), device_id_type=MESH)
    pl.semaphore_signal(barrier, inc=1, device_id=mate, device_id_type=MESH)
    for cp in own_dir:
        cp.wait()
    pl.semaphore_wait(barrier, len(greet) + 1)

    first = [[new() for k in range(4)] for h in range(2)]
    for d, dz in plane:
        send(first[0][d], own[0], own[0], peer(d, 0, dz), True)
        send(first[1][d], own[1], own[1], peer(0, d, dz), True)
    for h in range(2):
        for d in range(4):
            sent(first[h][d], g.at[c, h, pl.ds(0, 3 if d == 0 else 4)])

    ids_m = new()
    send(ids_m, ids_h, idm_v, mate)
    for cp in ret_l:
        cp.wait()
    ret_m = new()
    send(ret_m, ret, rxr, mate)

    rx_por[8] = jnp.zeros_like(rx_por[8])
    por[8] = jnp.zeros_like(por[8])

    ds_l.wait()
    res_l.wait()

    w = dot(ds[...], res[...])
    a0[...] = w
    a0b[...] = w.astype(BF16)
    recv(ret_m, rxr)
    for i in range(4):
        kall[y, rank, z, i] = ret[c * 4 + i] * rxr[c * 4 + i]
    kz_m = [new() for k in range(3)]
    for k in (2, 1, 3):
        send(kz_m[k - 1], kall.at[y, rank, z], kall.at[y, rank, z], peer(0, 0, k))

    ci_l.wait()

    m1[...] = dot(ds[...], ci[...]).astype(BF16)
    own_line = (xs, ys)
    second = [[new() for k in range(3)] for h in range(2)]

    def line(h, v, d):
        return g.at[c, h, pl.ds((v * 4 + own_line[h][-d % 4]) * 4, 4)]

    def third(h, k):
        return peer(0, k, 0) if h == 0 else peer(k, 0, 0)

    me = (y, x)
    for d in (0, 1, 3, 2):
        for h in range(2):
            if d == 0:
                recv(first[h][0], g.at[c, h, pl.ds(0, 3)])
            else:
                recv(first[h][d], line(h, me[h], d))
            for k in (2, 1, 3):
                send(second[h][k - 1], line(h, me[h], d), line(h, me[h], d), third(h, k), True)
    across = (ys, xs)

    def block(p, h, v):
        return g.at[p, h, pl.ds(v * 16, 16)]

    for h in range(2):
        for k in range(3):
            sent(second[h][k], block(c, h, 0))
    onchip = [[new() for k in range(4)] for h in range(2)]
    for h in range(2):
        send(onchip[h][0], block(c, h, me[h]), block(c, h, me[h]), mate)


    for k in (1, 3, 2):
        recv(kz_m[k - 1], kall.at[y, rank, zs[-k % 4]])
    kx_m = [new() for k in range(3)]
    for k in (2, 1, 3):
        send(kx_m[k - 1], kall.at[y, rank], kall.at[y, rank], peer(k, 0, 0))

    cs_l.wait()

    def turn(src, dst):
        def tile(i, u):
            q = pl.ds(pl.multiple_of(i * 128, 128), 128)
            dst[q, :] = src[:, q].T
            return u

        lax.fori_loop(0, 8, tile, 0)

    def turn_by_core(i, u):
        t = ci[:, pl.ds(pl.multiple_of(i * 128, 128), 128)].T
        for zl in range(2):
            for q in range(2):
                row = pl.multiple_of(q * 512 + i * 64 + zl * 32, 32)
                cit[pl.ds(row, 32), :] = t[zl * 64 + q * 32 : zl * 64 + q * 32 + 32]
        return u

    turn(cs, cst)
    lax.fori_loop(0, 8, turn_by_core, 0)

    def product_half(p, left, to, const):
        to[half(p), :] = dot(left[half(p), :], m1[...]).astype(BF16)
        const[half(p), :] = dot(left[half(p), :], a0b[...])

    def half(p):
        return pl.ds(pl.multiple_of(p * 512, 512), 512)

    product_half(oc, cst, b, ca)
    b_m, ca_m, pm_m, pa_m = new(), new(), new(), new()
    send(b_m, b.at[half(oc)], bm, mate)
    send(ca_m, ca.at[half(oc)], cam, mate)
    product_half(oc, cit, pm, pa)
    send(pm_m, pm.at[half(oc)], pmm, mate)
    send(pa_m, pa.at[half(oc)], pam, mate)
    for k in (1, 3, 2):
        recv(kx_m[k - 1], kall.at[y, x_rank[-k % 4]])
    ky_m = [new() for k in range(3)]
    for k in (2, 1, 3):
        send(ky_m[k - 1], kall.at[y], kall.at[y], peer(0, k, 0))

    for k in (1, 3):
        for h in range(2):
            v = across[h][-k % 4]
            recv(second[h][k - 1], block(c, h, v))
            send(onchip[h][k], block(c, h, v), block(c, h, v), mate)


    for h in range(2):
        v = across[h][2]
        recv(second[h][1], block(c, h, v))
        send(onchip[h][2], block(c, h, v), block(c, h, v), mate)


    product_half(c, cst, b, ca)
    product_half(c, cit, pm, pa)

    ids_l.wait()
    recv(ids_m, idm_v)
    load(idm_v, idm_s).wait()

    def place_of(n, u):
        for who, listed in ((0, ids_s), (1, idm_s)):
            found = jnp.int32(8)
            for k in range(LINKS):
                found = jnp.where(listed[0, k] == n, jnp.int32(k), found)
            table[who, n] = found
        return u

    lax.fori_loop(0, BLOCKS, place_of, 0)

    def column(i, v):
        col[i] = jnp.broadcast_to(v, (128, 128)).T

    for i in range(4):
        r_own, r_mate = ret[c * 4 + i], rxr[c * 4 + i]
        r0 = jnp.where(c == 0, r_own, r_mate)
        r1 = jnp.where(c == 0, r_mate, r_own)
        one = jnp.ones_like(r1)
        column(i, r0)
        column(4 + i, jnp.where(c == 0, r1, one))
        column(8 + i, jnp.where(c == 0, one, r1))

    for k in (1, 3, 2):
        recv(ky_m[k - 1], kall.at[ys[-k % 4]])
    for i in range(64):
        kmat[0, i : i + 1, :] = kall[i // 16, i // 4 % 4, i % 4, y]
    kmat[0, 64:128, :] = jnp.zeros((64, 128), F32)
    kmat[1] = kmat[0].T
    mine = kmat[1, pl.ds(pl.multiple_of((rank * 2 + lax.div(z, 2)) * 16, 16), 16), :]
    for i in range(64):
        kcol[i] = jnp.broadcast_to(mine[:, i : i + 1], (16, 128))
    total = None
    for i in range(8):
        v = kcol[i * 8]
        for j in range(1, 8):
            v = v * kcol[i * 8 + j]
        kseg[i] = v
        total = v if total is None else total * v
    kseg[8] = 1.0 / (1.0 - total)

    for k in (0, 1, 3, 2):
        for h in range(2):
            recv(onchip[h][k], block(oc, h, across[h][-k % 4]))

    def pick(k, u):
        for who, listed in ((0, ids_s), (1, idm_s)):
            pick_block(k, who, listed[0, k])
        return u

    def pick_block(k, who, n):
        py, pr, zh = lax.div(n, 8), lax.rem(lax.div(n, 2), 4), lax.rem(n, 2)
        px = lax.rem(pr, 2) * 2 + lax.div(pr, 2)
        for zl in range(2):
            where = ((py * 4 + px) * 4 + zh * 2 + zl, (px * 4 + py) * 4 + zh * 2 + zl)
            for q in range(2):
                for h in range(2):
                    row = pl.multiple_of(k * 128 + zl * 64 + q * 32 + h * 16, 16)
                    picked[who, pl.ds(row, 16), :] = g[q, h, where[h]]

    lax.fori_loop(0, LINKS, pick, 0)

    recv(b_m, bm)
    recv(ca_m, cam)
    own_i[...] = ca[half(c), :] - dot(b[half(c), :], picked[0])
    rx_i[...] = cam[...] - dot(bm[...], picked[1])
    for i in range(4):
        r = pl.ds(i * 128, 128)
        for q in range(2):
            w = pl.ds(q * 128, 128)
            mine, theirs = own_i[r, w], rx_i[r, w]
            v = (col[4 + i] * mine + col[8 + i] * theirs).astype(BF16)
            for j in range(8):
                tx_p[(i * 8 + j) * 2 + q] = v[j * 16 : (j + 1) * 16]
            day0[r, w] = jnp.where(c == 0, mine, theirs)
    year_m = new()
    for d in flat:
        send(year_m, tx_p.at[year(*d)], rx_p.at[here], peer(*d), True)
    sent(year_m, rx_p.at[pl.ds(0, 63)])
    rx_p[here] = tx_p[here]


    recv(pm_m, pmm)
    recv(pa_m, pam)
    v = pa[half(c), :] - dot(pm[half(c), :], picked[0])
    por[pl.ds(0, 8)] = v.astype(BF16).reshape(8, 2, 2, 16, 256)
    v = pam[...] - dot(pmm[...], picked[1])
    rx_por[pl.ds(0, 8)] = v.astype(BF16).reshape(8, 2, 2, 16, 256)

    def spread(n, u):
        v = por[table[0, n]] + rx_por[table[1, n]]
        py, pr, zh = lax.div(n, 8), lax.rem(lax.div(n, 2), 4), lax.rem(n, 2)
        px = lax.rem(pr, 2) * 2 + lax.div(pr, 2)
        for zl in range(2):
            s[0, px, py, zh * 2 + zl] = v[zl, 0]
            s[1, py, px, zh * 2 + zl] = v[zl, 1]
        return u

    lax.fori_loop(0, BLOCKS, spread, 0)

    r1_m = [[new() for k in range(3)] for h in range(2)]
    for k in (2, 1, 3):
        for h in range(2):
            to = peer(k, 0, 0) if h == 0 else peer(0, k, 0)
            send(r1_m[h][k - 1], s.at[h, (xs, ys)[h][k]], full.at[h, k - 1], to)

    def solve_tile(i, u):
        r = pl.ds(pl.multiple_of(i * 512, 512), 512)
        solved[r, :] = (a0[r, :] - dot(m1[r, :], picked[0])).astype(BF16)
        return u

    lax.fori_loop(0, 2, solve_tile, 0)

    w = dot(ds[...], cs[...]).astype(BF16)
    m2[0] = w[:, 0:512]
    m2[1] = w[:, 512:1024]

    recv(year_m, rx_p.at[pl.ds(0, 63)])
    runs = []
    for i in range(8):
        v = rx_p[i * 8].astype(F32)
        for j in range(1, 8):
            v = kcol[i * 8 + j] * v + rx_p[i * 8 + j].astype(F32)
        runs.append(v)
    v = runs[0]
    for i in range(1, 8):
        v = kseg[i] * v + runs[i]
    v = v * kseg[8]
    starts = []
    for i in range(8):
        starts.append(v)
        v = kseg[i] * v + runs[i]
    for i in range(8):
        v = starts[i]
        for j in range(8):
            tx_c[i * 8 + j] = v.astype(BF16)
            if j < 7:
                v = kcol[i * 8 + j] * v + rx_p[i * 8 + j].astype(F32)
    back_m = new()
    for d in flat:
        send(back_m, tx_c.at[year(*d)], rx_c.at[here], peer(*d), True)
    sent(back_m, rx_c.at[pl.ds(0, 63)])
    rx_c[here] = tx_c[here]


    r2_m = [new() for h in range(2)]
    for h in range(2):
        v = s[h, me[1 - h]].astype(F32)
        for k in (1, 3, 2):
            recv(r1_m[h][k - 1], full.at[h, k - 1])
            v = v + full[h, k - 1].astype(F32)
        t1[h] = v.astype(BF16)
        for d, dz in plane:
            to = peer(0, d, dz) if h == 0 else peer(d, 0, dz)
            send(r2_m[h], t1.at[h, across[h][d], zs[dz]], rx2.at[h, d * 4 + dz], to, True)
        sent(r2_m[h], rx2.at[h, pl.ds(1, 15)])


    recv(back_m, rx_c.at[pl.ds(0, 63)])
    for i in range(4):
        for j in range(8):
            for q in range(2):
                a = i * 128 + j * 16
                r, w = pl.ds(a, 16), pl.ds(q * 128, 128)
                u = rx_c[(i * 8 + j) * 2 + q].astype(F32)
                v = col[i, j * 16 : (j + 1) * 16, :] * u + day0[r, w]
                state[c, r, w] = jnp.where(c == 0, u, v).astype(BF16)
                tx_s[r, w] = jnp.where(c == 0, v, u).astype(BF16)
    swap_m = new()
    send(swap_m, tx_s, state.at[c], mate)

    def back_own(i, u):
        r = pl.ds(pl.multiple_of(i * 512, 512), 512)
        a0[r, :] = solved[r, :].astype(F32) - dot(m2[c, r, :], state[c])
        return u

    lax.fori_loop(0, 2, back_own, 0)

    for h in range(2):
        recv(r2_m[h], rx2.at[h, pl.ds(1, 15)])
        v = t1[h, me[h], z].astype(F32)
        for k in range(1, 16):
            v = v + rx2[h, k].astype(F32)
        inv_v[h * 16 : (h + 1) * 16, :] = v * SCALE

    recv(swap_m, state.at[oc])
    for i in range(2):
        r = pl.ds(i * 512, 512)
        du_v[r, :] = (a0[r, :] - dot(m2[oc, r, :], state[oc])).astype(BF16)

    for cp in sends:
        cp.wait_send()


def body(*arrays):
    hbm = pl.BlockSpec(memory_space=pl.ANY)
    v = pltpu.VMEM
    scratch = [
        v((1024, 1024), BF16), v((1024, 1024), BF16), v((1024, 1024), BF16), v((1024, 256), BF16),
        v((1024, 1024), BF16), v((1024, 1024), BF16), v((1024, 1024), BF16), v((2, 1024, 512), BF16),
        v((1024, 256), F32), v((1024, 256), BF16), v((1024, 1024), BF16), v((512, 1024), BF16), v((1024, 256), F32), v((512, 256), F32),
        v((1024, 1024), BF16), v((512, 1024), BF16), v((1024, 256), F32), v((512, 256), F32),
        v((2, 2, 64, 16, 256), BF16), v((2, 1024, 256), BF16), v((1024, 256), BF16),
        pltpu.SMEM((1, 8), jnp.int32), pltpu.SMEM((1, 8), jnp.int32), v((1, 8), jnp.int32),
        pltpu.SMEM((2, 32), jnp.int32),
        v((8, 1, 128), F32), v((8, 1, 128), F32), v((4, 4, 4, 4, 1, 128), F32),
        v((2, 128, 128), F32), v((64, 16, 128), F32), v((9, 16, 128), F32), v((12, 128, 128), F32),
        v((512, 256), F32), v((512, 256), F32), v((512, 256), F32),
        v((64, 16, 128), BF16), v((64, 16, 128), BF16), v((64, 16, 128), BF16), v((64, 16, 128), BF16),
        v((512, 256), BF16),
        v((9, 2, 2, 16, 256), BF16), v((9, 2, 2, 16, 256), BF16), v((2, 4, 4, 4, 16, 256), BF16),
        v((2, 3, 4, 4, 16, 256), BF16), v((2, 4, 4, 16, 256), BF16), v((2, 16, 16, 256), BF16),
        pltpu.SemaphoreType.DMA((32,)), pltpu.SemaphoreType.DMA((MESSAGES,)), pltpu.SemaphoreType.DMA((MESSAGES,)),
    ]
    inv, state, du = pl.pallas_call(
        kernel,
        out_shape=(v((32, 256), F32), v((2, 512, 256), BF16), v((1024, 256), BF16)),
        in_specs=[hbm] * 7,
        out_specs=(pl.BlockSpec(memory_space=v),) * 3,
        scratch_shapes=scratch,
        compiler_params=pltpu.CompilerParams(
            collective_id=0, has_side_effects=True, vmem_limit_bytes=60 * 1024 * 1024
        ),
    )(*arrays)
    return pl.pallas_call(
        deliver,
        out_shape=(
            jax.ShapeDtypeStruct((32, 256), F32),
            jax.ShapeDtypeStruct((1, 1024, 256), BF16),
            jax.ShapeDtypeStruct((1, 1024, 256), BF16),
        ),
        in_specs=[pl.BlockSpec(memory_space=v)] * 3,
        out_specs=(hbm,) * 3,
        scratch_shapes=[pltpu.SemaphoreType.DMA((4,))],
        compiler_params=pltpu.CompilerParams(vmem_limit_bytes=8 * 1024 * 1024),
    )(inv, state, du)


def deliver(inv_v, state, du_v, inv_o, st_o, du_o, sem):
    cps = [
        pltpu.make_async_copy(state.at[0], st_o.at[0, pl.ds(0, 512), :], sem.at[0]),
        pltpu.make_async_copy(state.at[1], st_o.at[0, pl.ds(512, 512), :], sem.at[1]),
        pltpu.make_async_copy(du_v, du_o.at[0], sem.at[2]),
        pltpu.make_async_copy(inv_v, inv_o, sem.at[3]),
    ]
    for cp in cps:
        cp.start()
    for cp in cps:
        cp.wait()


def solution(mesh):
    days = ("sec", "blk")
    in_specs = (
        P(days, None, None), P(days, None, None), P(days, None), P(days, None, None),
        P(days, None, None), P(days, None), P(days, None),
    )
    out_specs = (P(days, None), P(days, None, None), P(days, None, None))
    return jax.shard_map(body, mesh=mesh, in_specs=in_specs, out_specs=out_specs, check_vma=False)
```

```python
import jax
import jax.numpy as jnp
from jax import lax
from jax.experimental import pallas as pl
from jax.experimental.pallas import tpu as pltpu
from jax.sharding import PartitionSpec as P

MESH = pl.DeviceIdType.MESH
F32 = jnp.float32
BF16 = jnp.bfloat16
BLOCKS = 32
LINKS = 8
DAYS = 128
SCALE = (BLOCKS / (DAYS * LINKS)) ** 0.5
MESSAGES = 96


def dot(a, b):
    return jnp.dot(a, b, preferred_element_type=F32)


def kernel(
    ds_h, ci_h, ids_h, cs_h, res_h, dir_h, ret_h,
    inv_v, state, du_v,
    ds, ci, cs, res, cit, cst, m1, m2, a0, a0b, b, bm, ca, cam, pm, pmm, pa, pam, ga, gb, picked, solved,
    ids_s, idm_s, idm_v, table,
    ret, rxr, kall, kmat, kcol, kseg, col,
    own_i, rx_i, day0, tx_p, rx_p, tx_c, rx_c, tx_s,
    por, rx_por, sa, sb, full_a, full_b, t1_a, t1_b, rx2_a, rx2_b,
    lsem, ssem, rsem,
):
    sec, blk = lax.axis_index("sec"), lax.axis_index("blk")
    y, x_lo = lax.div(sec, 2), lax.rem(sec, 2)
    x_hi, z, c = lax.div(blk, 8), lax.rem(lax.div(blk, 2), 4), lax.rem(blk, 2)
    x = x_hi * 2 + x_lo
    rank = x_lo * 2 + x_hi
    oc = 1 - c
    here = (y * 4 + rank) * 4 + z

    xs, ys, zs = ([lax.rem(v + k, 4) for k in range(4)] for v in (x, y, z))
    x_sec, x_blk = [lax.rem(v, 2) for v in xs], [lax.div(v, 2) * 8 + c for v in xs]
    y_sec, z_blk = [v * 2 for v in ys], [v * 2 for v in zs]
    x_rank = [lax.rem(v, 2) * 2 + lax.div(v, 2) for v in xs]
    x_at, y_at = [v * 4 for v in x_rank], [v * 16 for v in ys]

    def peer(dx, dy, dz):
        return (y_sec[dy % 4] + x_sec[dx % 4], x_blk[dx % 4] + z_blk[dz % 4])

    def year(dx, dy, dz):
        return y_at[dy % 4] + x_at[dx % 4] + zs[dz % 4]

    x_only = [v - c for v in x_blk]
    p_sec, q_sec = [a + c * (b - a) for a, b in zip(y_sec, x_sec)], [b + c * (a - b) for a, b in zip(y_sec, x_sec)]
    p_blk, q_blk = [c * b for b in x_only], [oc * b for b in x_only]
    coord = {
        "p": [a + c * (b - a) for a, b in zip(ys, xs)], "q": [b + c * (a - b) for a, b in zip(ys, xs)], "z": zs,
    }

    axes = (("p", "q", "z"), ("q", "p", "z"), ("z", "q", "p"))

    def to(u, own_k, line_k, minor_k):
        k = dict(zip(axes[u], (own_k, line_k, minor_k)))
        p, q, r = k["p"] % 4, k["q"] % 4, k["z"] % 4
        return (p_sec[p] + q_sec[q], p_blk[p] + q_blk[q] + c + z_blk[r])

    def at(u, which, k):
        return coord[axes[u][which]][k % 4]

    def far(d):
        return -sum(min(v, 4 - v) for v in d)

    mate = (sec, blk + 1 - 2 * c)
    count = [0]
    sends = []
    local = [0]

    def new():
        count[0] += 1
        return count[0] - 1

    def copy(m, src, dst, to):
        return pltpu.make_async_remote_copy(
            src_ref=src, dst_ref=dst, send_sem=ssem.at[m], recv_sem=rsem.at[m],
            device_id=to, device_id_type=MESH,
        )

    def send(m, src, dst, to, whole=None):
        cp = copy(m, src, dst, to)
        cp.start()
        if whole is None:
            sends.append(cp)

    def sent(m, whole):
        sends.append(copy(m, whole, whole, mate))

    def recv(m, dst):
        copy(m, dst, dst, mate).wait_recv()

    def load(src, dst):
        cp = pltpu.make_async_copy(src, dst, lsem.at[local[0]])
        local[0] += 1
        cp.start()
        return cp

    def gather(par, u):
        return ga.at[par] if u == 0 else gb.at[par, u - 1]

    own = [gather(c, u).at[(at(u, 0, 0) * 4 + at(u, 1, 0)) * 4 + at(u, 2, 0)] for u in range(3)]
    own_dir = [
        load(dir_h.at[pl.ds(0, 16)], own[0]),
        load(dir_h.at[pl.ds(16, 16), pl.ds(0, 128)], own[1]),
        load(dir_h.at[pl.ds(16, 16), pl.ds(128, 128)], own[2]),
    ]
    ret_l = [load(ret_h.at[:, pl.ds(i * 128, 128)], ret.at[i]) for i in range(8)]
    ids_l = load(ids_h, ids_s)
    ds_l = load(ds_h.at[0], ds)
    res_l = load(res_h.at[0], res)
    ci_l = load(ci_h.at[0], ci)
    cs_l = load(cs_h.at[0], cs)

    plane = sorted([(i, j) for i in range(4) for j in range(4) if i or j], key=far)
    flat = sorted(
        [(i, j, k) for i in range(4) for j in range(4) for k in range(4) if i or j or k], key=far
    )
    greet = [d for d in flat if 0 in d]
    barrier = pltpu.get_barrier_semaphore()
    for d in greet:
        pl.semaphore_signal(barrier, inc=1, device_id=peer(*d), device_id_type=MESH)
    pl.semaphore_signal(barrier, inc=1, device_id=mate, device_id_type=MESH)
    for cp in own_dir:
        cp.wait()
    pl.semaphore_wait(barrier, len(greet) + 1)

    first = [[new() for k in range(4)] for u in range(3)]
    for dl, dm in plane:
        for u in range(3):
            send(first[u][dl], own[u], own[u], to(u, 0, dl, dm), True)
    for u in range(3):
        for k in range(4):
            sent(first[u][k], gather(c, u).at[pl.ds(0, 3 if k == 0 else 4)])

    ids_m = new()
    send(ids_m, ids_h, idm_v, mate)
    for cp in ret_l:
        cp.wait()
    ret_m = new()
    send(ret_m, ret, rxr, mate)

    rx_por[8] = jnp.zeros_like(rx_por[8])
    por[8] = jnp.zeros_like(por[8])

    ds_l.wait()
    res_l.wait()

    w = dot(ds[...], res[...])
    a0[...] = w
    a0b[...] = w.astype(BF16)
    recv(ret_m, rxr)
    for i in range(4):
        kall[y, rank, z, i] = ret[c * 4 + i] * rxr[c * 4 + i]
    kz_m = [new() for k in range(3)]
    for k in (2, 1, 3):
        send(kz_m[k - 1], kall.at[y, rank, z], kall.at[y, rank, z], peer(0, 0, k))

    ci_l.wait()

    m1[...] = dot(ds[...], ci[...]).astype(BF16)
    second = [[new() for k in range(3)] for u in range(3)]

    def line(u, d):
        return gather(c, u).at[pl.ds((at(u, 0, 0) * 4 + at(u, 1, -d)) * 4, 4)]

    for d in (0, 1, 3, 2):
        for u in range(3):
            recv(first[u][d], gather(c, u).at[pl.ds(0, 3)] if d == 0 else line(u, d))
            for k in (2, 1, 3):
                send(second[u][k - 1], line(u, d), line(u, d), to(u, k, 0, 0), True)

    def block(p, u, v):
        return gather(p, u).at[pl.ds(v * 16, 16)]

    for u in range(3):
        for k in range(3):
            sent(second[u][k], block(c, u, 0))
    onchip = [[new() for k in range(4)] for u in range(3)]
    for u in range(3):
        send(onchip[u][0], block(c, u, at(u, 0, 0)), block(c, u, at(u, 0, 0)), mate)

    for k in (1, 3, 2):
        recv(kz_m[k - 1], kall.at[y, rank, zs[-k % 4]])
    kx_m = [new() for k in range(3)]
    for k in (2, 1, 3):
        send(kx_m[k - 1], kall.at[y, rank], kall.at[y, rank], peer(k, 0, 0))

    cs_l.wait()

    def turn(src, dst):
        def tile(i, u):
            q = pl.ds(pl.multiple_of(i * 128, 128), 128)
            dst[q, :] = src[:, q].T
            return u

        lax.fori_loop(0, 8, tile, 0)

    def turn_by_core(i, u):
        t = ci[:, pl.ds(pl.multiple_of(i * 128, 128), 128)].T
        for zl in range(2):
            for q in range(2):
                row = pl.multiple_of(q * 512 + i * 64 + zl * 32, 32)
                cit[pl.ds(row, 32), :] = t[zl * 64 + q * 32 : zl * 64 + q * 32 + 32]
        return u

    turn(cs, cst)
    lax.fori_loop(0, 8, turn_by_core, 0)

    def product_half(p, left, to, const):
        to[half(p), :] = dot(left[half(p), :], m1[...]).astype(BF16)
        const[half(p), :] = dot(left[half(p), :], a0b[...])

    def half(p):
        return pl.ds(pl.multiple_of(p * 512, 512), 512)

    product_half(oc, cst, b, ca)
    b_m, ca_m, pm_m, pa_m = new(), new(), new(), new()
    send(b_m, b.at[half(oc)], bm, mate)
    send(ca_m, ca.at[half(oc)], cam, mate)
    product_half(oc, cit, pm, pa)
    send(pm_m, pm.at[half(oc)], pmm, mate)
    send(pa_m, pa.at[half(oc)], pam, mate)
    for k in (1, 3, 2):
        recv(kx_m[k - 1], kall.at[y, x_rank[-k % 4]])
    ky_m = [new() for k in range(3)]
    for k in (2, 1, 3):
        send(ky_m[k - 1], kall.at[y], kall.at[y], peer(0, k, 0))

    for k in (1, 3, 2):
        for u in range(3):
            v = at(u, 0, -k)
            recv(second[u][k - 1], block(c, u, v))
            send(onchip[u][k], block(c, u, v), block(c, u, v), mate)

    product_half(c, cst, b, ca)
    product_half(c, cit, pm, pa)

    ids_l.wait()
    recv(ids_m, idm_v)
    load(idm_v, idm_s).wait()

    def place_of(n, u):
        for who, listed in ((0, ids_s), (1, idm_s)):
            found = jnp.int32(8)
            for k in range(LINKS):
                found = jnp.where(listed[0, k] == n, jnp.int32(k), found)
            table[who, n] = found
        return u

    lax.fori_loop(0, BLOCKS, place_of, 0)

    def column(i, v):
        col[i] = jnp.broadcast_to(v, (128, 128)).T

    for i in range(4):
        r_own, r_mate = ret[c * 4 + i], rxr[c * 4 + i]
        r0 = jnp.where(c == 0, r_own, r_mate)
        r1 = jnp.where(c == 0, r_mate, r_own)
        one = jnp.ones_like(r1)
        column(i, r0)
        column(4 + i, jnp.where(c == 0, r1, one))
        column(8 + i, jnp.where(c == 0, one, r1))

    for k in (1, 3, 2):
        recv(ky_m[k - 1], kall.at[ys[-k % 4]])
    for i in range(64):
        kmat[0, i : i + 1, :] = kall[i // 16, i // 4 % 4, i % 4, y]
    kmat[0, 64:128, :] = jnp.zeros((64, 128), F32)
    kmat[1] = kmat[0].T
    mine = kmat[1, pl.ds(pl.multiple_of((rank * 2 + lax.div(z, 2)) * 16, 16), 16), :]
    for i in range(64):
        kcol[i] = jnp.broadcast_to(mine[:, i : i + 1], (16, 128))
    total = None
    for i in range(8):
        v = kcol[i * 8]
        for j in range(1, 8):
            v = v * kcol[i * 8 + j]
        kseg[i] = v
        total = v if total is None else total * v
    kseg[8] = 1.0 / (1.0 - total)

    for k in (0, 1, 3, 2):
        for u in range(3):
            recv(onchip[u][k], block(oc, u, at(u, 0, -k)))

    def pick(k, u):
        for who, listed in ((0, ids_s), (1, idm_s)):
            pick_block(k, who, listed[0, k])
        return u

    def pick_block(k, who, n):
        py, pr, zh = lax.div(n, 8), lax.rem(lax.div(n, 2), 4), lax.rem(n, 2)
        px = lax.rem(pr, 2) * 2 + lax.div(pr, 2)
        for zl in range(2):
            pz = zh * 2 + zl
            for q in range(2):
                a, b = (py, px) if q == 0 else (px, py)
                row = pl.multiple_of(k * 128 + zl * 64 + q * 32, 16)
                picked[who, pl.ds(row, 16), :] = ga[q, (a * 4 + b) * 4 + pz]
                row = pl.multiple_of(row + 16, 16)
                picked[who, pl.ds(row, 16), 0:128] = gb[q, 0, (b * 4 + a) * 4 + pz]
                picked[who, pl.ds(row, 16), 128:256] = gb[q, 1, (pz * 4 + b) * 4 + a]

    lax.fori_loop(0, LINKS, pick, 0)

    recv(b_m, bm)
    recv(ca_m, cam)
    own_i[...] = ca[half(c), :] - dot(b[half(c), :], picked[0])
    rx_i[...] = cam[...] - dot(bm[...], picked[1])
    for i in range(4):
        r = pl.ds(i * 128, 128)
        for q in range(2):
            w = pl.ds(q * 128, 128)
            mine, theirs = own_i[r, w], rx_i[r, w]
            v = (col[4 + i] * mine + col[8 + i] * theirs).astype(BF16)
            for j in range(8):
                tx_p[(i * 8 + j) * 2 + q] = v[j * 16 : (j + 1) * 16]
            day0[r, w] = jnp.where(c == 0, mine, theirs)
    year_m = new()
    for d in flat:
        send(year_m, tx_p.at[year(*d)], rx_p.at[here], peer(*d), True)
    sent(year_m, rx_p.at[pl.ds(0, 63)])
    rx_p[here] = tx_p[here]


    recv(pm_m, pmm)
    recv(pa_m, pam)
    v = pa[half(c), :] - dot(pm[half(c), :], picked[0])
    por[pl.ds(0, 8)] = v.astype(BF16).reshape(8, 2, 2, 16, 256)
    v = pam[...] - dot(pmm[...], picked[1])
    rx_por[pl.ds(0, 8)] = v.astype(BF16).reshape(8, 2, 2, 16, 256)

    def spread(n, u):
        v = por[table[0, n]] + rx_por[table[1, n]]
        py, pr, zh = lax.div(n, 8), lax.rem(lax.div(n, 2), 4), lax.rem(n, 2)
        px = lax.rem(pr, 2) * 2 + lax.div(pr, 2)
        pp, pq = py + c * (px - py), px + c * (py - px)
        for zl in range(2):
            pz = zh * 2 + zl
            sa[pp, pq, pz] = v[zl, 0]
            sb[0, pq, pp, pz] = v[zl, 1, :, 0:128]
            sb[1, pz, pq, pp] = v[zl, 1, :, 128:256]
        return u

    lax.fori_loop(0, BLOCKS, spread, 0)

    def pick_ref(u, a, b):
        return a if u == 0 else b.at[u - 1]

    parts = [pick_ref(u, sa, sb) for u in range(3)]
    full = [pick_ref(u, full_a, full_b) for u in range(3)]
    t1 = [pick_ref(u, t1_a, t1_b) for u in range(3)]
    rx2 = [pick_ref(u, rx2_a, rx2_b) for u in range(3)]
    r1_m = [[new() for k in range(3)] for u in range(3)]
    for k in (2, 1, 3):
        for u in range(3):
            send(r1_m[u][k - 1], parts[u].at[at(u, 0, k)], full[u].at[k - 1], to(u, k, 0, 0))

    def solve_tile(i, u):
        r = pl.ds(pl.multiple_of(i * 512, 512), 512)
        solved[r, :] = (a0[r, :] - dot(m1[r, :], picked[0])).astype(BF16)
        return u

    lax.fori_loop(0, 2, solve_tile, 0)

    w = dot(ds[...], cs[...]).astype(BF16)
    m2[0] = w[:, 0:512]
    m2[1] = w[:, 512:1024]

    recv(year_m, rx_p.at[pl.ds(0, 63)])
    runs = []
    for i in range(8):
        v = rx_p[i * 8].astype(F32)
        for j in range(1, 8):
            v = kcol[i * 8 + j] * v + rx_p[i * 8 + j].astype(F32)
        runs.append(v)
    v = runs[0]
    for i in range(1, 8):
        v = kseg[i] * v + runs[i]
    v = v * kseg[8]
    starts = []
    for i in range(8):
        starts.append(v)
        v = kseg[i] * v + runs[i]
    for i in range(8):
        v = starts[i]
        for j in range(8):
            tx_c[i * 8 + j] = v.astype(BF16)
            if j < 7:
                v = kcol[i * 8 + j] * v + rx_p[i * 8 + j].astype(F32)
    back_m = new()
    for d in flat:
        send(back_m, tx_c.at[year(*d)], rx_c.at[here], peer(*d), True)
    sent(back_m, rx_c.at[pl.ds(0, 63)])
    rx_c[here] = tx_c[here]


    r2_m = [new() for u in range(3)]
    for u in range(3):
        v = parts[u][at(u, 0, 0)].astype(F32)
        for k in (1, 3, 2):
            recv(r1_m[u][k - 1], full[u].at[k - 1])
            v = v + full[u][k - 1].astype(F32)
        t1[u][...] = v.astype(BF16)
        for dl, dm in plane:
            send(
                r2_m[u], t1[u].at[at(u, 1, dl), at(u, 2, dm)], rx2[u].at[dl * 4 + dm], to(u, 0, dl, dm), True
            )
        sent(r2_m[u], rx2[u].at[pl.ds(1, 15)])

    recv(back_m, rx_c.at[pl.ds(0, 63)])
    swap_m = [new() for i in range(4)]
    for i in range(4):
        for j in range(8):
            for q in range(2):
                a = i * 128 + j * 16
                r, w = pl.ds(a, 16), pl.ds(q * 128, 128)
                u = rx_c[(i * 8 + j) * 2 + q].astype(F32)
                v = col[i, j * 16 : (j + 1) * 16, :] * u + day0[r, w]
                state[c, r, w] = jnp.where(c == 0, u, v).astype(BF16)
                tx_s[r, w] = jnp.where(c == 0, v, u).astype(BF16)
        r = pl.ds(i * 128, 128)
        send(swap_m[i], tx_s.at[r], state.at[c, r], mate)

    def back_own(i, u):
        r = pl.ds(pl.multiple_of(i * 512, 512), 512)
        a0[r, :] = solved[r, :].astype(F32) - dot(m2[c, r, :], state[c])
        return u

    lax.fori_loop(0, 2, back_own, 0)

    for u in range(3):
        recv(r2_m[u], rx2[u].at[pl.ds(1, 15)])
        v = t1[u][at(u, 1, 0), at(u, 2, 0)].astype(F32)
        for k in range(1, 16):
            v = v + rx2[u][k].astype(F32)
        v = v * SCALE
        if u == 0:
            inv_v[0:16, :] = v
        else:
            inv_v[16:32, (u - 1) * 128 : u * 128] = v

    for i in range(4):
        recv(swap_m[i], state.at[oc, pl.ds(i * 128, 128)])
    for i in range(2):
        r = pl.ds(i * 512, 512)
        du_v[r, :] = (a0[r, :] - dot(m2[oc, r, :], state[oc])).astype(BF16)

    for cp in sends:
        cp.wait_send()


def body(*arrays):
    hbm = pl.BlockSpec(memory_space=pl.ANY)
    v = pltpu.VMEM
    scratch = [
        v((1024, 1024), BF16), v((1024, 1024), BF16), v((1024, 1024), BF16), v((1024, 256), BF16),
        v((1024, 1024), BF16), v((1024, 1024), BF16), v((1024, 1024), BF16), v((2, 1024, 512), BF16),
        v((1024, 256), F32), v((1024, 256), BF16), v((1024, 1024), BF16), v((512, 1024), BF16), v((1024, 256), F32), v((512, 256), F32),
        v((1024, 1024), BF16), v((512, 1024), BF16), v((1024, 256), F32), v((512, 256), F32),
        v((2, 64, 16, 256), BF16), v((2, 2, 64, 16, 128), BF16), v((2, 1024, 256), BF16), v((1024, 256), BF16),
        pltpu.SMEM((1, 8), jnp.int32), pltpu.SMEM((1, 8), jnp.int32), v((1, 8), jnp.int32),
        pltpu.SMEM((2, 32), jnp.int32),
        v((8, 1, 128), F32), v((8, 1, 128), F32), v((4, 4, 4, 4, 1, 128), F32),
        v((2, 128, 128), F32), v((64, 16, 128), F32), v((9, 16, 128), F32), v((12, 128, 128), F32),
        v((512, 256), F32), v((512, 256), F32), v((512, 256), F32),
        v((64, 16, 128), BF16), v((64, 16, 128), BF16), v((64, 16, 128), BF16), v((64, 16, 128), BF16),
        v((512, 256), BF16),
        v((9, 2, 2, 16, 256), BF16), v((9, 2, 2, 16, 256), BF16),
        v((4, 4, 4, 16, 256), BF16), v((2, 4, 4, 4, 16, 128), BF16),
        v((3, 4, 4, 16, 256), BF16), v((2, 3, 4, 4, 16, 128), BF16),
        v((4, 4, 16, 256), BF16), v((2, 4, 4, 16, 128), BF16),
        v((16, 16, 256), BF16), v((2, 16, 16, 128), BF16),
        pltpu.SemaphoreType.DMA((32,)), pltpu.SemaphoreType.DMA((MESSAGES,)), pltpu.SemaphoreType.DMA((MESSAGES,)),
    ]
    inv, state, du = pl.pallas_call(
        kernel,
        out_shape=(v((32, 256), F32), v((2, 512, 256), BF16), v((1024, 256), BF16)),
        in_specs=[hbm] * 7,
        out_specs=(pl.BlockSpec(memory_space=v),) * 3,
        scratch_shapes=scratch,
        compiler_params=pltpu.CompilerParams(
            collective_id=0, has_side_effects=True, vmem_limit_bytes=60 * 1024 * 1024
        ),
    )(*arrays)
    return pl.pallas_call(
        deliver,
        out_shape=(
            jax.ShapeDtypeStruct((32, 256), F32),
            jax.ShapeDtypeStruct((1, 1024, 256), BF16),
            jax.ShapeDtypeStruct((1, 1024, 256), BF16),
        ),
        in_specs=[pl.BlockSpec(memory_space=v)] * 3,
        out_specs=(hbm,) * 3,
        scratch_shapes=[pltpu.SemaphoreType.DMA((4,))],
        compiler_params=pltpu.CompilerParams(vmem_limit_bytes=8 * 1024 * 1024),
    )(inv, state, du)


def deliver(inv_v, state, du_v, inv_o, st_o, du_o, sem):
    cps = [
        pltpu.make_async_copy(state.at[0], st_o.at[0, pl.ds(0, 512), :], sem.at[0]),
        pltpu.make_async_copy(state.at[1], st_o.at[0, pl.ds(512, 512), :], sem.at[1]),
        pltpu.make_async_copy(du_v, du_o.at[0], sem.at[2]),
        pltpu.make_async_copy(inv_v, inv_o, sem.at[3]),
    ]
    for cp in cps:
        cp.start()
    for cp in cps:
        cp.wait()


def solution(mesh):
    days = ("sec", "blk")
    in_specs = (
        P(days, None, None), P(days, None, None), P(days, None), P(days, None, None),
        P(days, None, None), P(days, None), P(days, None),
    )
    out_specs = (P(days, None), P(days, None, None), P(days, None, None))
    return jax.shard_map(body, mesh=mesh, in_specs=in_specs, out_specs=out_specs, check_vma=False)
```

```python
import jax
import jax.numpy as jnp
from jax import lax
from jax.experimental import pallas as pl
from jax.experimental.pallas import tpu as pltpu
from jax.sharding import PartitionSpec as P

MESH = pl.DeviceIdType.MESH
F32 = jnp.float32
BF16 = jnp.bfloat16
BLOCKS = 32
LINKS = 8
DAYS = 128
SCALE = (BLOCKS / (DAYS * LINKS)) ** 0.5
MESSAGES = 96


def dot(a, b):
    return jnp.dot(a, b, preferred_element_type=F32)


def kernel(
    ds_h, ci_h, ids_h, cs_h, res_h, dir_h, ret_h,
    inv_v, state, du_v,
    ds, ci, cs, res, cit, m1, m2, a0, a0b, b, bm, ca, cam, pm, pmm, pa, pam, ga, gb, picked, solved,
    ids_s, idm_s, idm_v, table,
    ret, rxr, kall, kmat, kcol, kseg, col,
    own_i, rx_i, day0, tx_p, rx_p, tx_c, rx_c, tx_s,
    por, rx_por, sa, sb, full_a, full_b, t1_a, t1_b, rx2_a, rx2_b,
    lsem, ssem, rsem,
):
    sec, blk = lax.axis_index("sec"), lax.axis_index("blk")
    y, x_lo = lax.div(sec, 2), lax.rem(sec, 2)
    x_hi, z, c = lax.div(blk, 8), lax.rem(lax.div(blk, 2), 4), lax.rem(blk, 2)
    x = x_hi * 2 + x_lo
    rank = x_lo * 2 + x_hi
    oc = 1 - c
    here = (y * 4 + rank) * 4 + z

    xs, ys, zs = ([lax.rem(v + k, 4) for k in range(4)] for v in (x, y, z))
    x_sec, x_blk = [lax.rem(v, 2) for v in xs], [lax.div(v, 2) * 8 + c for v in xs]
    y_sec, z_blk = [v * 2 for v in ys], [v * 2 for v in zs]
    x_rank = [lax.rem(v, 2) * 2 + lax.div(v, 2) for v in xs]
    x_at, y_at = [v * 4 for v in x_rank], [v * 16 for v in ys]

    def peer(dx, dy, dz):
        return (y_sec[dy % 4] + x_sec[dx % 4], x_blk[dx % 4] + z_blk[dz % 4])

    def year(dx, dy, dz):
        return y_at[dy % 4] + x_at[dx % 4] + zs[dz % 4]

    x_only = [v - c for v in x_blk]
    p_sec, q_sec = [a + c * (b - a) for a, b in zip(y_sec, x_sec)], [b + c * (a - b) for a, b in zip(y_sec, x_sec)]
    p_blk, q_blk = [c * b for b in x_only], [oc * b for b in x_only]
    coord = {
        "p": [a + c * (b - a) for a, b in zip(ys, xs)], "q": [b + c * (a - b) for a, b in zip(ys, xs)], "z": zs,
    }

    axes = (("p", "q", "z"), ("q", "p", "z"), ("z", "q", "p"))

    def to(u, own_k, line_k, minor_k):
        k = dict(zip(axes[u], (own_k, line_k, minor_k)))
        p, q, r = k["p"] % 4, k["q"] % 4, k["z"] % 4
        return (p_sec[p] + q_sec[q], p_blk[p] + q_blk[q] + c + z_blk[r])

    def at(u, which, k):
        return coord[axes[u][which]][k % 4]

    def far(d):
        return -sum(min(v, 4 - v) for v in d)

    mate = (sec, blk + 1 - 2 * c)
    count = [0]
    sends = []
    local = [0]

    def new():
        count[0] += 1
        return count[0] - 1

    def copy(m, src, dst, to):
        return pltpu.make_async_remote_copy(
            src_ref=src, dst_ref=dst, send_sem=ssem.at[m], recv_sem=rsem.at[m],
            device_id=to, device_id_type=MESH,
        )

    def send(m, src, dst, to, whole=None):
        cp = copy(m, src, dst, to)
        cp.start()
        if whole is None:
            sends.append(cp)

    def sent(m, whole):
        sends.append(copy(m, whole, whole, mate))

    def recv(m, dst):
        copy(m, dst, dst, mate).wait_recv()

    def load(src, dst):
        cp = pltpu.make_async_copy(src, dst, lsem.at[local[0]])
        local[0] += 1
        cp.start()
        return cp

    def gather(par, u):
        return ga.at[par] if u == 0 else gb.at[par, u - 1]

    own = [gather(c, u).at[(at(u, 0, 0) * 4 + at(u, 1, 0)) * 4 + at(u, 2, 0)] for u in range(3)]
    own_dir = [
        load(dir_h.at[pl.ds(0, 16)], own[0]),
        load(dir_h.at[pl.ds(16, 16), pl.ds(0, 128)], own[1]),
        load(dir_h.at[pl.ds(16, 16), pl.ds(128, 128)], own[2]),
    ]
    ret_l = [load(ret_h.at[:, pl.ds(i * 128, 128)], ret.at[i]) for i in range(8)]
    ids_l = load(ids_h, ids_s)
    ds_l = load(ds_h.at[0], ds)
    res_l = load(res_h.at[0], res)
    ci_l = load(ci_h.at[0], ci)
    cs_l = load(cs_h.at[0], cs)

    plane = sorted([(i, j) for i in range(4) for j in range(4) if i or j], key=far)
    flat = sorted(
        [(i, j, k) for i in range(4) for j in range(4) for k in range(4) if i or j or k], key=far
    )
    greet = [d for d in flat if 0 in d]
    barrier = pltpu.get_barrier_semaphore()
    for d in greet:
        pl.semaphore_signal(barrier, inc=1, device_id=peer(*d), device_id_type=MESH)
    pl.semaphore_signal(barrier, inc=1, device_id=mate, device_id_type=MESH)
    for cp in own_dir:
        cp.wait()
    pl.semaphore_wait(barrier, len(greet) + 1)

    first = [[new() for k in range(4)] for u in range(3)]
    for dl, dm in plane:
        for u in range(3):
            send(first[u][dl], own[u], own[u], to(u, 0, dl, dm), True)
    for u in range(3):
        for k in range(4):
            sent(first[u][k], gather(c, u).at[pl.ds(0, 3 if k == 0 else 4)])

    ids_m = new()
    send(ids_m, ids_h, idm_v, mate)
    for cp in ret_l:
        cp.wait()
    ret_m = new()
    send(ret_m, ret, rxr, mate)

    rx_por[8] = jnp.zeros_like(rx_por[8])
    por[8] = jnp.zeros_like(por[8])

    ds_l.wait()
    res_l.wait()

    w = dot(ds[...], res[...])
    a0[...] = w
    a0b[...] = w.astype(BF16)
    recv(ret_m, rxr)
    for i in range(4):
        kall[y, rank, z, i] = ret[c * 4 + i] * rxr[c * 4 + i]
    kz_m = [new() for k in range(3)]
    for k in (2, 1, 3):
        send(kz_m[k - 1], kall.at[y, rank, z], kall.at[y, rank, z], peer(0, 0, k))

    ci_l.wait()

    m1[...] = dot(ds[...], ci[...]).astype(BF16)
    second = [[new() for k in range(3)] for u in range(3)]

    def line(u, d):
        return gather(c, u).at[pl.ds((at(u, 0, 0) * 4 + at(u, 1, -d)) * 4, 4)]

    for d in (0, 1, 3, 2):
        for u in range(3):
            recv(first[u][d], gather(c, u).at[pl.ds(0, 3)] if d == 0 else line(u, d))
            for k in (2, 1, 3):
                send(second[u][k - 1], line(u, d), line(u, d), to(u, k, 0, 0), True)

    def block(p, u, v):
        return gather(p, u).at[pl.ds(v * 16, 16)]

    for u in range(3):
        for k in range(3):
            sent(second[u][k], block(c, u, 0))
    onchip = [[new() for k in range(4)] for u in range(3)]
    for u in range(3):
        send(onchip[u][0], block(c, u, at(u, 0, 0)), block(c, u, at(u, 0, 0)), mate)

    for k in (1, 3, 2):
        recv(kz_m[k - 1], kall.at[y, rank, zs[-k % 4]])
    kx_m = [new() for k in range(3)]
    for k in (2, 1, 3):
        send(kx_m[k - 1], kall.at[y, rank], kall.at[y, rank], peer(k, 0, 0))

    cs_l.wait()

    def turn_by_core(i, u):
        t = ci[:, pl.ds(pl.multiple_of(i * 128, 128), 128)].T
        for zl in range(2):
            for q in range(2):
                row = pl.multiple_of(q * 512 + i * 64 + zl * 32, 32)
                cit[pl.ds(row, 32), :] = t[zl * 64 + q * 32 : zl * 64 + q * 32 + 32]
        return u

    lax.fori_loop(0, 8, turn_by_core, 0)

    def product_half(p, left, to, const):
        to[half(p), :] = dot(left[half(p), :], m1[...]).astype(BF16)
        const[half(p), :] = dot(left[half(p), :], a0b[...])

    def turned(a, b):
        return lax.dot_general(a, b, (((0,), (0,)), ((), ())), preferred_element_type=F32)

    def push_half(p):
        left = cs[:, half(p)]
        b[half(p), :] = turned(left, m1[...]).astype(BF16)
        ca[half(p), :] = turned(left, a0b[...])

    def half(p):
        return pl.ds(pl.multiple_of(p * 512, 512), 512)

    push_half(oc)
    b_m, ca_m, pm_m, pa_m = new(), new(), new(), new()
    send(b_m, b.at[half(oc)], bm, mate)
    send(ca_m, ca.at[half(oc)], cam, mate)
    product_half(oc, cit, pm, pa)
    send(pm_m, pm.at[half(oc)], pmm, mate)
    send(pa_m, pa.at[half(oc)], pam, mate)
    for k in (1, 3, 2):
        recv(kx_m[k - 1], kall.at[y, x_rank[-k % 4]])
    ky_m = [new() for k in range(3)]
    for k in (2, 1, 3):
        send(ky_m[k - 1], kall.at[y], kall.at[y], peer(0, k, 0))

    for k in (1, 3, 2):
        for u in range(3):
            v = at(u, 0, -k)
            recv(second[u][k - 1], block(c, u, v))
            send(onchip[u][k], block(c, u, v), block(c, u, v), mate)

    push_half(c)
    product_half(c, cit, pm, pa)

    ids_l.wait()
    recv(ids_m, idm_v)
    load(idm_v, idm_s).wait()

    def place_of(n, u):
        for who, listed in ((0, ids_s), (1, idm_s)):
            found = jnp.int32(8)
            for k in range(LINKS):
                found = jnp.where(listed[0, k] == n, jnp.int32(k), found)
            table[who, n] = found
        return u

    lax.fori_loop(0, BLOCKS, place_of, 0)

    def column(i, v):
        col[i] = jnp.broadcast_to(v, (128, 128)).T

    for i in range(4):
        r_own, r_mate = ret[c * 4 + i], rxr[c * 4 + i]
        r0 = jnp.where(c == 0, r_own, r_mate)
        r1 = jnp.where(c == 0, r_mate, r_own)
        one = jnp.ones_like(r1)
        column(i, r0)
        column(4 + i, jnp.where(c == 0, r1, one))
        column(8 + i, jnp.where(c == 0, one, r1))

    for k in (0, 1, 3, 2):
        for u in range(3):
            recv(onchip[u][k], block(oc, u, at(u, 0, -k)))

    def pick(k, u):
        for who, listed in ((0, ids_s), (1, idm_s)):
            pick_block(k, who, listed[0, k])
        return u

    def pick_block(k, who, n):
        py, pr, zh = lax.div(n, 8), lax.rem(lax.div(n, 2), 4), lax.rem(n, 2)
        px = lax.rem(pr, 2) * 2 + lax.div(pr, 2)
        for zl in range(2):
            pz = zh * 2 + zl
            for q in range(2):
                a, b = (py, px) if q == 0 else (px, py)
                row = pl.multiple_of(k * 128 + zl * 64 + q * 32, 16)
                picked[who, pl.ds(row, 16), :] = ga[q, (a * 4 + b) * 4 + pz]
                row = pl.multiple_of(row + 16, 16)
                picked[who, pl.ds(row, 16), 0:128] = gb[q, 0, (b * 4 + a) * 4 + pz]
                picked[who, pl.ds(row, 16), 128:256] = gb[q, 1, (pz * 4 + b) * 4 + a]

    lax.fori_loop(0, LINKS, pick, 0)

    recv(b_m, bm)
    recv(ca_m, cam)
    own_i[...] = ca[half(c), :] - dot(b[half(c), :], picked[0])
    rx_i[...] = cam[...] - dot(bm[...], picked[1])
    for i in range(4):
        r = pl.ds(i * 128, 128)
        for q in range(2):
            w = pl.ds(q * 128, 128)
            mine, theirs = own_i[r, w], rx_i[r, w]
            v = (col[4 + i] * mine + col[8 + i] * theirs).astype(BF16)
            for j in range(8):
                tx_p[(i * 8 + j) * 2 + q] = v[j * 16 : (j + 1) * 16]
            day0[r, w] = jnp.where(c == 0, mine, theirs)
    year_m = new()
    for d in flat:
        send(year_m, tx_p.at[year(*d)], rx_p.at[here], peer(*d), True)
    sent(year_m, rx_p.at[pl.ds(0, 63)])
    rx_p[here] = tx_p[here]


    recv(pm_m, pmm)
    recv(pa_m, pam)
    v = pa[half(c), :] - dot(pm[half(c), :], picked[0])
    por[pl.ds(0, 8)] = v.astype(BF16).reshape(8, 2, 2, 16, 256)
    v = pam[...] - dot(pmm[...], picked[1])
    rx_por[pl.ds(0, 8)] = v.astype(BF16).reshape(8, 2, 2, 16, 256)

    def spread(n, u):
        v = por[table[0, n]] + rx_por[table[1, n]]
        py, pr, zh = lax.div(n, 8), lax.rem(lax.div(n, 2), 4), lax.rem(n, 2)
        px = lax.rem(pr, 2) * 2 + lax.div(pr, 2)
        pp, pq = py + c * (px - py), px + c * (py - px)
        for zl in range(2):
            pz = zh * 2 + zl
            sa[pp, pq, pz] = v[zl, 0]
            sb[0, pq, pp, pz] = v[zl, 1, :, 0:128]
            sb[1, pz, pq, pp] = v[zl, 1, :, 128:256]
        return u

    lax.fori_loop(0, BLOCKS, spread, 0)

    def pick_ref(u, a, b):
        return a if u == 0 else b.at[u - 1]

    parts = [pick_ref(u, sa, sb) for u in range(3)]
    full = [pick_ref(u, full_a, full_b) for u in range(3)]
    t1 = [pick_ref(u, t1_a, t1_b) for u in range(3)]
    rx2 = [pick_ref(u, rx2_a, rx2_b) for u in range(3)]
    r1_m = [[new() for k in range(3)] for u in range(3)]
    for k in (2, 1, 3):
        for u in range(3):
            send(r1_m[u][k - 1], parts[u].at[at(u, 0, k)], full[u].at[k - 1], to(u, k, 0, 0))

    for k in (1, 3, 2):
        recv(ky_m[k - 1], kall.at[ys[-k % 4]])
    for i in range(64):
        kmat[0, i : i + 1, :] = kall[i // 16, i // 4 % 4, i % 4, y]
    kmat[0, 64:128, :] = jnp.zeros((64, 128), F32)
    kmat[1] = kmat[0].T
    mine = kmat[1, pl.ds(pl.multiple_of((rank * 2 + lax.div(z, 2)) * 16, 16), 16), :]
    for i in range(64):
        kcol[i] = jnp.broadcast_to(mine[:, i : i + 1], (16, 128))
    total = None
    for i in range(8):
        v = kcol[i * 8]
        for j in range(1, 8):
            v = v * kcol[i * 8 + j]
        kseg[i] = v
        total = v if total is None else total * v
    kseg[8] = 1.0 / (1.0 - total)

    w = dot(ds[...], cs[...]).astype(BF16)
    m2[0] = w[:, 0:512]
    m2[1] = w[:, 512:1024]

    recv(year_m, rx_p.at[pl.ds(0, 63)])
    runs = []
    for i in range(8):
        v = rx_p[i * 8].astype(F32)
        for j in range(1, 8):
            v = kcol[i * 8 + j] * v + rx_p[i * 8 + j].astype(F32)
        runs.append(v)
    v = runs[0]
    for i in range(1, 8):
        v = kseg[i] * v + runs[i]
    v = v * kseg[8]
    starts = []
    for i in range(8):
        starts.append(v)
        v = kseg[i] * v + runs[i]
    for i in range(8):
        v = starts[i]
        for j in range(8):
            tx_c[i * 8 + j] = v.astype(BF16)
            if j < 7:
                v = kcol[i * 8 + j] * v + rx_p[i * 8 + j].astype(F32)
    back_m = new()
    for d in flat:
        send(back_m, tx_c.at[year(*d)], rx_c.at[here], peer(*d), True)
    sent(back_m, rx_c.at[pl.ds(0, 63)])
    rx_c[here] = tx_c[here]


    r2_m = [new() for u in range(3)]
    for u in range(3):
        v = parts[u][at(u, 0, 0)].astype(F32)
        for k in (1, 3, 2):
            recv(r1_m[u][k - 1], full[u].at[k - 1])
            v = v + full[u][k - 1].astype(F32)
        t1[u][...] = v.astype(BF16)
        for dl, dm in plane:
            send(
                r2_m[u], t1[u].at[at(u, 1, dl), at(u, 2, dm)], rx2[u].at[dl * 4 + dm], to(u, 0, dl, dm), True
            )
        sent(r2_m[u], rx2[u].at[pl.ds(1, 15)])

    def solve_tile(i, u):
        r = pl.ds(pl.multiple_of(i * 512, 512), 512)
        solved[r, :] = (a0[r, :] - dot(m1[r, :], picked[0])).astype(BF16)
        return u

    lax.fori_loop(0, 2, solve_tile, 0)

    recv(back_m, rx_c.at[pl.ds(0, 63)])
    swap_m = [new() for i in range(4)]
    for i in range(4):
        for j in range(8):
            for q in range(2):
                a = i * 128 + j * 16
                r, w = pl.ds(a, 16), pl.ds(q * 128, 128)
                u = rx_c[(i * 8 + j) * 2 + q].astype(F32)
                v = col[i, j * 16 : (j + 1) * 16, :] * u + day0[r, w]
                state[c, r, w] = jnp.where(c == 0, u, v).astype(BF16)
                tx_s[r, w] = jnp.where(c == 0, v, u).astype(BF16)
        r = pl.ds(i * 128, 128)
        send(swap_m[i], tx_s.at[r], state.at[c, r], mate)

    def back_own(i, u):
        r = pl.ds(pl.multiple_of(i * 512, 512), 512)
        a0[r, :] = solved[r, :].astype(F32) - dot(m2[c, r, :], state[c])
        return u

    lax.fori_loop(0, 2, back_own, 0)

    for u in range(3):
        recv(r2_m[u], rx2[u].at[pl.ds(1, 15)])
        v = t1[u][at(u, 1, 0), at(u, 2, 0)].astype(F32)
        for k in range(1, 16):
            v = v + rx2[u][k].astype(F32)
        v = v * SCALE
        if u == 0:
            inv_v[0:16, :] = v
        else:
            inv_v[16:32, (u - 1) * 128 : u * 128] = v

    for i in range(4):
        recv(swap_m[i], state.at[oc, pl.ds(i * 128, 128)])
    for i in range(2):
        r = pl.ds(i * 512, 512)
        du_v[r, :] = (a0[r, :] - dot(m2[oc, r, :], state[oc])).astype(BF16)

    for cp in sends:
        cp.wait_send()


def body(*arrays):
    hbm = pl.BlockSpec(memory_space=pl.ANY)
    v = pltpu.VMEM
    scratch = [
        v((1024, 1024), BF16), v((1024, 1024), BF16), v((1024, 1024), BF16), v((1024, 256), BF16),
        v((1024, 1024), BF16), v((1024, 1024), BF16), v((2, 1024, 512), BF16),
        v((1024, 256), F32), v((1024, 256), BF16), v((1024, 1024), BF16), v((512, 1024), BF16), v((1024, 256), F32), v((512, 256), F32),
        v((1024, 1024), BF16), v((512, 1024), BF16), v((1024, 256), F32), v((512, 256), F32),
        v((2, 64, 16, 256), BF16), v((2, 2, 64, 16, 128), BF16), v((2, 1024, 256), BF16), v((1024, 256), BF16),
        pltpu.SMEM((1, 8), jnp.int32), pltpu.SMEM((1, 8), jnp.int32), v((1, 8), jnp.int32),
        pltpu.SMEM((2, 32), jnp.int32),
        v((8, 1, 128), F32), v((8, 1, 128), F32), v((4, 4, 4, 4, 1, 128), F32),
        v((2, 128, 128), F32), v((64, 16, 128), F32), v((9, 16, 128), F32), v((12, 128, 128), F32),
        v((512, 256), F32), v((512, 256), F32), v((512, 256), F32),
        v((64, 16, 128), BF16), v((64, 16, 128), BF16), v((64, 16, 128), BF16), v((64, 16, 128), BF16),
        v((512, 256), BF16),
        v((9, 2, 2, 16, 256), BF16), v((9, 2, 2, 16, 256), BF16),
        v((4, 4, 4, 16, 256), BF16), v((2, 4, 4, 4, 16, 128), BF16),
        v((3, 4, 4, 16, 256), BF16), v((2, 3, 4, 4, 16, 128), BF16),
        v((4, 4, 16, 256), BF16), v((2, 4, 4, 16, 128), BF16),
        v((16, 16, 256), BF16), v((2, 16, 16, 128), BF16),
        pltpu.SemaphoreType.DMA((32,)), pltpu.SemaphoreType.DMA((MESSAGES,)), pltpu.SemaphoreType.DMA((MESSAGES,)),
    ]
    inv, state, du = pl.pallas_call(
        kernel,
        out_shape=(v((32, 256), F32), v((2, 512, 256), BF16), v((1024, 256), BF16)),
        in_specs=[hbm] * 7,
        out_specs=(pl.BlockSpec(memory_space=v),) * 3,
        scratch_shapes=scratch,
        compiler_params=pltpu.CompilerParams(
            collective_id=0, has_side_effects=True, vmem_limit_bytes=60 * 1024 * 1024
        ),
    )(*arrays)
    return pl.pallas_call(
        deliver,
        out_shape=(
            jax.ShapeDtypeStruct((32, 256), F32),
            jax.ShapeDtypeStruct((1, 1024, 256), BF16),
            jax.ShapeDtypeStruct((1, 1024, 256), BF16),
        ),
        in_specs=[pl.BlockSpec(memory_space=v)] * 3,
        out_specs=(hbm,) * 3,
        scratch_shapes=[pltpu.SemaphoreType.DMA((4,))],
        compiler_params=pltpu.CompilerParams(vmem_limit_bytes=8 * 1024 * 1024),
    )(inv, state, du)


def deliver(inv_v, state, du_v, inv_o, st_o, du_o, sem):
    cps = [
        pltpu.make_async_copy(state.at[0], st_o.at[0, pl.ds(0, 512), :], sem.at[0]),
        pltpu.make_async_copy(state.at[1], st_o.at[0, pl.ds(512, 512), :], sem.at[1]),
        pltpu.make_async_copy(du_v, du_o.at[0], sem.at[2]),
        pltpu.make_async_copy(inv_v, inv_o, sem.at[3]),
    ]
    for cp in cps:
        cp.start()
    for cp in cps:
        cp.wait()


def solution(mesh):
    days = ("sec", "blk")
    in_specs = (
        P(days, None, None), P(days, None, None), P(days, None), P(days, None, None),
        P(days, None, None), P(days, None), P(days, None),
    )
    out_specs = (P(days, None), P(days, None, None), P(days, None, None))
    return jax.shard_map(body, mesh=mesh, in_specs=in_specs, out_specs=out_specs, check_vma=False)
```
